128 devices in a mesh: section: 2 (over z_hi), hid: 16 (over x, z_lo, core), wid: 4 (over y).
Axes of the slice: x: 4, y: 4, z: 4 (z_hi: 2, z_lo: 2; z = z_hi * 2 + z_lo), core: 2. Of those that a mesh axis runs over, the one named last changes fastest.
Arguments:
- grad_out: float32 [2, 256, 6144], P(None, None, 'wid'), may hold values from -6 to 6
- weight_in: bfloat16 [2, 6144, 24576], P('section', 'wid', 'hid'), may hold values from -0.078125 to 0.078125
- weight_out: bfloat16 [2, 24576, 6144], P('section', 'hid', 'wid'), may hold values from -0.0390625 to 0.0390625
- pre_act: float32 [2, 2, 256, 24576], P('section', None, None, 'hid'), may hold values from -6 to 6
Outputs:
- grads: float32 [2, 2, 256, 6144], P('section', None, None, 'wid')
The draws below stay inside these ranges and needn't reach their ends.
All inputs are finite; a program needn't handle non-finite values.
Results may differ from the reference program's by a relative error of at most 0.003.
Values may be sent and summed in bfloat16 or wider, within the bound.
A program may use at most 128 MiB of HBM per device.

```python
import jax
import jax.numpy as jnp
from jax import lax

D = 6144
FF = 24576
TOK = 256
MB = 2
N_HID = 16


def block_levels(key, extent, pieces, low, largest):
    level, own = 1.0, jax.random.fold_in(key, 6)
    for position, shards_of in pieces:
        steps = jnp.exp(jax.random.uniform(jax.random.fold_in(own, position), (shards_of,), jnp.float32, low / len(pieces), largest / len(pieces)))
        level = level * jnp.repeat(steps, extent[position] // shards_of).reshape([-1 if axis == position else 1 for axis in range(len(extent))])
    return level


def centred(rng, shape, spread, reach, split=(), dtype=jnp.bfloat16):
    array = jax.random.normal(rng, shape, jnp.float32) * spread
    if len(split) > 0:
        array = block_levels(rng, shape, split, -0.22, 0.18) * array
    return jnp.clip(array, min=-reach, max=reach).astype(dtype)


def setup_inputs(seed: int = 0) -> dict:
    splits = jax.random.split(jax.random.key(seed), 5)
    grad_out = centred(splits[0], (MB, TOK, D), 1.0, 6.0, ((2, 4),), jnp.float32)
    weight_in = centred(splits[1], (2, D, FF), D ** -0.5, 0.078125, ((0, 2), (1, 4), (2, 16)))
    weight_out = centred(splits[2], (2, FF, D), FF ** -0.5, 0.0390625, ((0, 2), (1, 16), (2, 4)))
    pre_act = centred(splits[3], (2, MB, TOK, FF), 1.5, 6.0, ((0, 2), (3, 16)), jnp.float32)
    return {"grad_out": grad_out, "weight_in": weight_in, "weight_out": weight_out, "pre_act": pre_act}


def gelu_slope(pre):
    normal_cdf = 0.5 * (1.0 + jax.scipy.special.erf(pre * 0.7071067811865476))
    density = jnp.exp(-0.5 * pre * pre) * 0.3989422804014327
    return normal_cdf + pre * density


def upstream_weights(weight_in, weight_out):
    tiles = N_HID
    narrow = FF // (2 * tiles)
    mat_in = weight_in[1].reshape(4, D // 4, tiles, FF // tiles).transpose(0, 2, 1, 3)
    mat_in = mat_in.reshape(2, 2, tiles, D // 2, narrow).transpose(0, 3, 2, 1, 4).reshape(D, FF)
    mat_out = weight_out[1].reshape(tiles, FF // tiles, 4, D // 4).transpose(0, 2, 1, 3)
    mat_out = mat_out.reshape(tiles, 2, 2, narrow, D // 2).transpose(0, 2, 3, 1, 4).reshape(FF, D)
    return mat_in, mat_out


def section_back(grad, tile_in, tile_out, pre):
    contract = (((1,), (1,)), ((), ()))
    hidden_grad = lax.dot_general(grad.astype(jnp.bfloat16), tile_out, contract, preferred_element_type=jnp.float32)
    hidden = (hidden_grad * gelu_slope(pre)).astype(jnp.bfloat16)
    return grad + lax.dot_general(hidden, tile_in, contract, preferred_element_type=jnp.float32)


def reference(grad_out, weight_in, weight_out, pre_act):
    up_in, up_out = upstream_weights(weight_in, weight_out)
    first = []
    second = []
    for batch_idx in range(MB):
        between = section_back(grad_out[batch_idx], weight_in[0], weight_out[0], pre_act[0, batch_idx])
        first.append(between)
        second.append(section_back(between, up_in, up_out, pre_act[1, batch_idx]))
    return jnp.stack([jnp.stack(first), jnp.stack(second)])
```

```python
import jax
import jax.numpy as jnp
from jax import lax
from jax.experimental import pallas as pl
from jax.experimental.pallas import tpu as pltpu
from jax.sharding import PartitionSpec as P

F32 = jnp.float32
BF16 = jnp.bfloat16
MESH = pl.DeviceIdType.MESH
N_REMOTE = 96
N_LOCAL = 24
NT = (((1,), (1,)), ((), ()))


def gelu_slope(pre):
    normal_cdf = 0.5 * (1.0 + lax.erf(pre * 0.7071067811865476))
    density = jnp.exp(-0.5 * pre * pre) * 0.3989422804014327
    return normal_cdf + pre * density


def dot_nt(a, b):
    return lax.dot_general(a, b, NT, preferred_element_type=F32)


def kernel(
    grad, win, wout, pre, out,
    v_raw, w_raw, v_nat, w_nat, stripe, gbuf, glow, prev, pa, r1, r2, hid, sb, rl, rp, pb, rc,
    xs, xr1, xr2, xsum, yr, ys, zr, bs, ob,
    send_sem, recv_sem, local_sem,
):
    s = lax.axis_index("section")
    h = lax.axis_index("hid")
    w = lax.axis_index("wid")
    x = lax.div(h, 4)
    zl = lax.rem(lax.div(h, 2), 2)
    core = lax.rem(h, 2)
    c = lax.div(w, 2)
    b = lax.rem(w, 2)
    zc = zl + s - 2 * zl * s
    batches, tok, tile = grad.shape
    half, fourth = tile // 2, tile // 4
    th, tq = tok // 2, tok // 4
    te = tq // 2

    def device(dx=0, dw=0, flip_core=False, flip_z=False, flip_s=False, flip_w=False):
        nx = lax.rem(x + dx + 4, 4) if dx else x
        nz = 1 - zl if flip_z else zl
        nc = 1 - core if flip_core else core
        nw = lax.rem(w + dw + 4, 4) if dw else w
        if flip_w:
            nw = w + 1 - 2 * b
        return {"section": 1 - s if flip_s else s, "hid": nx * 4 + nz * 2 + nc, "wid": nw}

    right, left = device(dx=1), device(dx=-1)
    up, down = device(dw=1), device(dw=-1)
    mate = device(flip_core=True)
    zmate = device(flip_z=True)
    cross = device(flip_s=True, flip_z=True)
    wmate = device(flip_w=True)

    keys = {}

    def remote(key, src, dst, to):
        index = keys.setdefault(key, len(keys))
        return pltpu.make_async_remote_copy(
            src_ref=src, dst_ref=dst, send_sem=send_sem.at[index], recv_sem=recv_sem.at[index],
            device_id=to, device_id_type=MESH,
        )

    local_keys = {}

    def local(key, src, dst):
        index = local_keys.setdefault(key, len(local_keys))
        return pltpu.make_async_copy(src, dst, local_sem.at[index])

    def of4(i):
        return lax.rem(i + 4, 4)

    def cols(start, size):
        return pl.ds(pl.multiple_of(start, size), size)

    started = []

    def send(copy):
        copy.start()
        started.append(copy)
        return copy

    pre_col = jnp.where(s == 0, fourth * w, half * b + fourth * c)
    pre_loads = [
        local(("pre", m), pre.at[0, m, :, cols(pre_col, fourth)], prev.at[m]) for m in range(batches)
    ]
    v_loads = [
        local(("v", r), wout.at[0, cols(fourth * of4(w + r), fourth), :],
              v_raw.at[cols(fourth * of4(w + r), fourth), :])
        for r in (2, 1, 3, 0)
    ]
    w_load = local("w", win.at[0], w_raw)
    g_loads = [local(("g", m), grad.at[m], gbuf.at[m]) for m in range(batches)]

    @pl.when(s == 0)
    def _():
        g_loads[0].start()

    for load in v_loads:
        load.start()
    for load in pre_loads:
        load.start()
    w_load.start()

    @pl.when(s == 0)
    def _():
        for load in g_loads[1:]:
            load.start()

    barrier = pltpu.get_barrier_semaphore()
    for peer in (right, left, up, down, mate, zmate, cross):
        pl.semaphore_signal(barrier, inc=1, device_id=peer, device_id_type=MESH)
    pl.semaphore_wait(barrier, 7)

    def slope_stage(m):
        pre_loads[m].wait()

        @pl.loop(0, 8)
        def _(i):
            rows = cols(i * (tok // 8), tok // 8)
            prev[m, rows, :] = gelu_slope(prev[m, rows, :])


    def core_send(m, q):
        return send(remote(("core", m, q), pb.at[m, q, 1 - core], rc.at[m, q], mate))

    def x_rows(r):
        return cols(tq * of4(x + r), tq)

    def chip_sum(m, q, r):
        rows = x_rows(r)
        return pb[m, q, core, rows, :] + rc[m, q, rows, :]

    def x_first(m, nq):
        for q in range(nq):
            xs[m, 0, q] = chip_sum(m, q, 2).astype(BF16)
        one = remote(("x1r", m), xs.at[m, 0, pl.ds(0, nq), pl.ds(0, te)], xr1.at[m, 0, pl.ds(0, nq)], right)
        two = remote(("x1l", m), xs.at[m, 0, pl.ds(0, nq), pl.ds(te, te)], xr1.at[m, 1, pl.ds(0, nq)], left)
        return send(one), send(two)

    def x_second(m, nq, first):
        result = []
        for side, (copy, r, to) in enumerate(((first[0], 1, right), (first[1], 3, left))):
            copy.wait_recv()
            lo = te * side
            for q in range(nq):
                total = chip_sum(m, q, r)
                xs[m, 1 + side, q] = total.astype(BF16)
                part = total[lo : lo + te] + xr1[m, side, q].astype(F32)
                xs[m, 1 + side, q, lo : lo + te] = part.astype(BF16)
            copy = remote(
                ("x2", m, side), xs.at[m, 1 + side, pl.ds(0, nq)], xr2.at[m, side, pl.ds(0, nq)], to
            )
            result.append(send(copy))
        return result

    def x_last(m, nq, second):
        for copy in second:
            copy.wait_recv()
        for q in range(nq):
            xsum[m, q] = chip_sum(m, q, 0) + xr2[m, 0, q].astype(F32) + xr2[m, 1, q].astype(F32)

    def z_stage(m):
        copy = send(remote(("z", m), ys.at[m, :, cols(fourth * (1 - zc), fourth)], zr.at[m], zmate))
        copy.wait_recv()
        return ys[m, :, cols(fourth * zc, fourth)] + zr[m]


    def shard_of(ref, m):
        return ref.at[m, core, cols(tq * x, tq), cols(fourth * zc, fourth)]

    def out_stage(m):
        first = send(remote(("oz", m), shard_of(ob, m), shard_of(ob, m), zmate))
        first.wait_recv()
        own = ob.at[m, core, cols(tq * x, tq)]
        to_right = send(remote(("ox1r", m), own, own, right))
        to_left = send(remote(("ox1l", m), own, own, left))
        to_right.wait_recv()
        piece = ob.at[m, core, cols(tq * of4(x - 1), te)]
        on_right = send(remote(("ox2r", m), piece, piece, right))
        to_left.wait_recv()
        piece = ob.at[m, core, cols(tq * of4(x + 1) + te, te)]
        on_left = send(remote(("ox2l", m), piece, piece, left))
        on_right.wait_recv()
        on_left.wait_recv()
        column = ob.at[m, core]
        last = send(remote(("oc", m), column, column, mate))
        mine = local(("om", m), column, out.at[0, m, :, cols(half * core, half)])
        mine.start()
        last.wait_recv()
        other = local(("oo", m), ob.at[m, 1 - core], out.at[0, m, :, cols(half * (1 - core), half)])
        other.start()
        return mine, other


    def down_hidden(m):
        g_loads[m].wait()
        for k in range(2):
            glow[m, 0, k] = gbuf[m, :, k * half : (k + 1) * half].astype(BF16)

        def partial(r):
            if m == 0:
                v_loads[(2, 1, 3, 0).index(r)].wait()
            rows = cols(fourth * of4(w + r), fourth)
            pa[m, r] = dot_nt(glow[m, 0, 0], v_raw[rows, :half]) + dot_nt(glow[m, 0, 1], v_raw[rows, half:])

        partial(2)
        one = send(remote(("a1u", m), pa.at[m, 2, pl.ds(0, th)], r1.at[m, 0], up))
        two = send(remote(("a1d", m), pa.at[m, 2, pl.ds(th, th)], r1.at[m, 1], down))
        partial(1)
        partial(3)
        one.wait_recv()
        pa[m, 1, :th] += r1[m, 0]
        three = send(remote(("a2u", m), pa.at[m, 1], r2.at[m, 0], up))
        two.wait_recv()
        pa[m, 3, th:] += r1[m, 1]
        four = send(remote(("a2d", m), pa.at[m, 3], r2.at[m, 1], down))
        partial(0)
        slope_stage(m)
        three.wait_recv()
        four.wait_recv()
        mine = cols(fourth * w, fourth)
        total = pa[m, 0] + r2[m, 0] + r2[m, 1]
        hid[m, :, mine] = (total * prev[m]).astype(BF16)
        own = hid.at[m, :, mine]
        to_up = send(remote(("h1u", m), own, own, up))
        to_down = send(remote(("h1d", m), own, own, down))
        to_up.wait_recv()
        piece = hid.at[m, pl.ds(0, th), cols(fourth * of4(w - 1), fourth)]
        on_up = send(remote(("h2u", m), piece, piece, up))
        to_down.wait_recv()
        piece = hid.at[m, pl.ds(th, th), cols(fourth * of4(w + 1), fourth)]
        on_down = send(remote(("h2d", m), piece, piece, down))
        on_up.wait_recv()
        on_down.wait_recv()

    def down_back(m):
        if m == 0:
            w_load.wait()

        def product(k):
            @pl.loop(0, 3)
            def _(n):
                rows = cols(half * k + (half // 3) * n, half // 3)
                pb[m, 0, k, :, cols((half // 3) * n, half // 3)] = dot_nt(hid[m], w_raw[rows, :])

        product(1 - core)
        copy = core_send(m, 0)
        product(core)
        copy.wait_recv()
        x_last(m, 1, x_second(m, 1, x_first(m, 1)))
        ys[m] = xsum[m, 0]
        total = z_stage(m)
        rows, columns = cols(tq * x, tq), cols(fourth * zc, fourth)
        ob[m, core, rows, columns] = total + gbuf[m, rows, cols(half * core + fourth * zc, fourth)]
        send(cross_copy(m))

    def cross_copy(m):
        return remote(("cross", m), shard_of(ob, m), bs.at[m], cross)

    @pl.when(s == 0)
    def _():
        for m in range(batches):
            down_hidden(m)
            down_back(m)
        last = []
        for m in range(batches):
            last += out_stage(m)
        for copy in last:
            copy.wait()
        for copy in started:
            copy.wait_send()

    started.clear()


    def up_weights():
        for load in v_loads:
            load.wait()

        @pl.loop(0, tile // 128)
        def _(i):
            columns = cols(128 * i, 128)
            stripe[:tile, :] = v_raw[:, columns].astype(F32)
            for q in range(2):
                v_nat[q, :, columns] = stripe[pl.ds(q, half, stride=2), :].astype(BF16)

        w_load.wait()

        @pl.loop(0, half // 128)
        def _(i):
            for q in range(2):
                stripe[pl.ds(q, tile, stride=2), :] = w_raw[:, cols(half * q + 128 * i, 128)].astype(F32)
            w_nat[:, cols(128 * i, 128)] = stripe[...].astype(BF16)

    def up_gather(m):
        cross_copy(m).wait_recv()
        rows, columns = cols(tq * x, tq), cols(fourth * zc, fourth)
        glow[m, b, core, rows, columns] = bs[m].astype(BF16)
        own = glow.at[m, b, core, rows, columns]
        copy = send(remote(("gw", m), own, own, wmate))
        copy.wait_recv()
        own = glow.at[m, :, core, rows, columns]
        copy = send(remote(("gz", m), own, own, zmate))
        copy.wait_recv()
        own = glow.at[m, :, core, rows]
        to_right = send(remote(("gx1r", m), own, own, right))
        to_left = send(remote(("gx1l", m), own, own, left))
        to_right.wait_recv()
        piece = glow.at[m, :, core, cols(tq * of4(x - 1), te)]
        on_right = send(remote(("gx2r", m), piece, piece, right))
        to_left.wait_recv()
        piece = glow.at[m, :, core, cols(tq * of4(x + 1) + te, te)]
        on_left = send(remote(("gx2l", m), piece, piece, left))
        on_right.wait_recv()
        on_left.wait_recv()
        column = glow.at[m, :, core]
        copy = send(remote(("gc", m), column, column, mate))
        copy.wait_recv()

    def opposite(name, m, src, dst, relays):
        one = send(remote((name, "1u", m), src.at[pl.ds(0, th)], relays.at[0], up))
        two = send(remote((name, "1d", m), src.at[pl.ds(th, th)], relays.at[1], down))
        one.wait_recv()
        three = send(remote((name, "2u", m), relays.at[0], dst(0, w - 1), up))
        two.wait_recv()
        four = send(remote((name, "2d", m), relays.at[1], dst(1, w + 1), down))
        three.wait_recv()
        four.wait_recv()

    def up_hidden(m):
        def partial(part):
            rows = cols(fourth * part, fourth)
            total = None
            for q in range(2):
                for k in range(2):
                    term = dot_nt(glow[m, q, k], v_nat[q, rows, k * half : (k + 1) * half])
                    total = term if total is None else total + term
            return total

        sb[m] = partial(1 - c).astype(BF16)
        pa[m, 0] = partial(c)
        opposite("p", m, sb.at[m], lambda side, _: rp.at[m, pl.ds(th * side, th)], rl.at[m, 0])
        mine = cols(fourth * c, fourth)
        total = pa[m, 0] + rp[m].astype(F32)
        hid[m, :, mine] = (total * prev[m]).astype(BF16)
        opposite(
            "h", m, hid.at[m, :, mine],
            lambda side, i: hid.at[m, pl.ds(th * side, th), cols(fourth * lax.div(of4(i), 2), fourth)],
            rl.at[m, 1],
        )

    def up_back(m):
        def product(q, k):
            @pl.loop(0, 3)
            def _(n):
                rows = cols(tile * q + half * k + (half // 3) * n, half // 3)
                pb[m, q, k, :, cols((half // 3) * n, half // 3)] = dot_nt(hid[m, :, :half], w_nat[rows, :])

        copies = []
        for q in range(2):
            product(q, 1 - core)
            copies.append(core_send(m, q))
        for q in range(2):
            product(q, core)
        for copy in copies:
            copy.wait_recv()
        x_last(m, 2, x_second(m, 2, x_first(m, 2)))
        copy = send(remote(("y", m), xsum.at[m, 1 - b], yr.at[m], wmate))
        copy.wait_recv()
        ys[m] = xsum[m, b] + yr[m]
        total = z_stage(m)
        rows, columns = cols(tq * x, tq), cols(fourth * zc, fourth)
        ob[m, core, rows, columns] = total + bs[m]

    @pl.when(s == 1)
    def _():
        up_weights()
        for m in range(batches):
            slope_stage(m)
        last = []
        for m in range(batches):
            up_gather(m)
            up_hidden(m)
            up_back(m)
            last += out_stage(m)
        for copy in last:
            copy.wait()
        for copy in started:
            copy.wait_send()


def local(grad_out, weight_in, weight_out, pre_act):
    batches, tok, tile = grad_out.shape
    half, fourth = tile // 2, tile // 4
    th, tq = tok // 2, tok // 4
    vmem = pltpu.VMEM
    scratch = [
        vmem((tile, tile), BF16),
        vmem((tile, tile), BF16),
        vmem((2, half, tile), BF16),
        vmem((2 * tile, half), BF16),
        vmem((2 * tile, 128), F32),
        vmem((batches, tok, tile), F32),
        vmem((batches, 2, 2, tok, half), BF16),
        vmem((batches, tok, fourth), F32),
        vmem((batches, 4, tok, fourth), F32),
        vmem((batches, 2, th, fourth), F32),
        vmem((batches, 2, tok, fourth), F32),
        vmem((batches, tok, tile), BF16),
        vmem((batches, tok, fourth), BF16),
        vmem((batches, 2, 2, th, fourth), BF16),
        vmem((batches, tok, fourth), BF16),
        vmem((batches, 2, 2, tok, half), F32),
        vmem((batches, 2, tok, half), F32),
        vmem((batches, 3, 2, tq, half), BF16),
        vmem((batches, 2, 2, tq // 2, half), BF16),
        vmem((batches, 2, 2, tq, half), BF16),
        vmem((batches, 2, tq, half), F32),
        vmem((batches, tq, half), F32),
        vmem((batches, tq, half), F32),
        vmem((batches, tq, fourth), F32),
        vmem((batches, tq, fourth), F32),
        vmem((batches, 2, tok, half), F32),
        pltpu.SemaphoreType.DMA((N_REMOTE,)),
        pltpu.SemaphoreType.DMA((N_REMOTE,)),
        pltpu.SemaphoreType.DMA((N_LOCAL,)),
    ]
    anywhere = pl.BlockSpec(memory_space=pl.ANY)
    return pl.pallas_call(
        kernel,
        out_shape=jax.ShapeDtypeStruct((1, batches, tok, tile), F32),
        in_specs=[anywhere] * 4,
        out_specs=anywhere,
        scratch_shapes=scratch,
        compiler_params=pltpu.CompilerParams(
            collective_id=0, has_side_effects=True, vmem_limit_bytes=67_000_000
        ),
    )(grad_out, weight_in, weight_out, pre_act)


def solution(mesh):
    return jax.shard_map(
        local,
        mesh=mesh,
        in_specs=(
            P(None, None, "wid"),
            P("section", "wid", "hid"),
            P("section", "hid", "wid"),
            P("section", None, None, "hid"),
        ),
        out_specs=P("section", None, None, "wid"),
        check_vma=False,
    )
```

```python
import jax
import jax.numpy as jnp
from jax import lax
from jax.experimental import pallas as pl
from jax.experimental.pallas import tpu as pltpu
from jax.sharding import PartitionSpec as P

F32 = jnp.float32
BF16 = jnp.bfloat16
MESH = pl.DeviceIdType.MESH
N_REMOTE = 240
N_LOCAL = 32
SPLIT = 2
START_DOWN = (0, 3, 5, 7)
START_UP = (0, 2, 4, 6)
NT = (((1,), (1,)), ((), ()))


def gelu_slope(pre):
    normal_cdf = 0.5 * (1.0 + lax.erf(pre * 0.7071067811865476))
    density = jnp.exp(-0.5 * pre * pre) * 0.3989422804014327
    return normal_cdf + pre * density


def dot_nt(a, b):
    return lax.dot_general(a, b, NT, preferred_element_type=F32)


def kernel(
    grad, win, wout, pre, out,
    v_raw, w_raw, v_nat, w_nat, stripe, gbuf, glow, gs, prev, pa, r1, r2, hid, pf, sb, rl, rp, pb, rc,
    xs, xr1, xr2, xsum, zr, bs, ob,
    send_sem, recv_sem, local_sem,
):
    s = lax.axis_index("section")
    h = lax.axis_index("hid")
    w = lax.axis_index("wid")
    x = lax.div(h, 4)
    zl = lax.rem(lax.div(h, 2), 2)
    core = lax.rem(h, 2)
    c = lax.div(w, 2)
    b = lax.rem(w, 2)
    zc = zl + s - 2 * zl * s
    tile = grad.shape[2]
    chunks, tok = pb.shape[0], pb.shape[3]
    half, fourth = tile // 2, tile // 4
    th, tq = tok // 2, tok // 4
    te = tq // 2

    def device(dx=0, dw=0, flip_core=False, flip_z=False, flip_s=False, flip_w=False):
        nx = lax.rem(x + dx + 4, 4) if dx else x
        nz = 1 - zl if flip_z else zl
        nc = 1 - core if flip_core else core
        nw = lax.rem(w + dw + 4, 4) if dw else w
        if flip_w:
            nw = w + 1 - 2 * b
        return {"section": 1 - s if flip_s else s, "hid": nx * 4 + nz * 2 + nc, "wid": nw}

    right, left = device(dx=1), device(dx=-1)
    up, down = device(dw=1), device(dw=-1)
    mate = device(flip_core=True)
    zmate = device(flip_z=True)
    wmate = device(flip_w=True)
    corner = device(flip_w=True, flip_z=True)
    cross = device(flip_s=True, flip_z=True)
    beyond = [
        device(flip_s=True), device(flip_s=True, flip_w=True), device(flip_s=True, flip_z=True, flip_w=True)
    ]

    keys = {}

    def remote(key, src, dst, to):
        index = keys.setdefault(key, len(keys))
        return pltpu.make_async_remote_copy(
            src_ref=src, dst_ref=dst, send_sem=send_sem.at[index], recv_sem=recv_sem.at[index],
            device_id=to, device_id_type=MESH,
        )

    local_keys = {}

    def local(key, src, dst):
        index = local_keys.setdefault(key, len(local_keys))
        return pltpu.make_async_copy(src, dst, local_sem.at[index])

    def of4(i):
        return lax.rem(i + 4, 4)

    def cols(start, size):
        return pl.ds(pl.multiple_of(start, size), size)

    started = []

    def send(copy):
        copy.start()
        started.append(copy)
        return copy


    def span(m):
        return m // SPLIT, pl.ds(tok * (m % SPLIT), tok)

    pre_down = [
        local(("pre", m), pre.at[(0, *span(m), cols(fourth * w, fourth))], prev.at[m, :, pl.ds(0, fourth)])
        for m in range(chunks)
    ]
    pre_up = [
        local(("pre", m), pre.at[(0, *span(m), cols(half * b, half))], prev.at[m]) for m in range(chunks)
    ]
    v_loads = [
        local(("v", r), wout.at[0, cols(fourth * of4(w + r), fourth), :],
              v_raw.at[cols(fourth * of4(w + r), fourth), :])
        for r in (2, 1, 3, 0)
    ]
    w_load = local("w", win.at[0], w_raw)
    g_loads = [local(("g", m), grad.at[span(m)], gbuf.at[m]) for m in range(chunks)]

    @pl.when(s == 0)
    def _():
        g_loads[0].start()

    for load in v_loads:
        load.start()
    w_load.start()

    @pl.when(s == 0)
    def _():
        for load in (*pre_down, *g_loads[1:]):
            load.start()

    @pl.when(s == 1)
    def _():
        for load in pre_up:
            load.start()

    barrier = pltpu.get_barrier_semaphore()
    peers = [right, left, up, down, mate, zmate, corner, cross, *beyond]
    for peer in peers:
        pl.semaphore_signal(barrier, inc=1, device_id=peer, device_id_type=MESH)
    pl.semaphore_wait(barrier, len(peers))

    def slope_stage(m, width):
        @pl.loop(0, 4)
        def _(i):
            rows = cols(i * (tok // 4), tok // 4)
            prev[m, rows, :width] = gelu_slope(prev[m, rows, :width])


    def core_send(m, q):
        return send(remote(("core", m, q), pb.at[m, q, 1 - core], rc.at[m, q], mate))

    def x_rows(r):
        return cols(tq * of4(x + r), tq)

    def chip_sum(m, q, r):
        rows = x_rows(r)
        return pb[m, q, core, rows, :] + rc[m, q, rows, :]

    def x_first(m, nq):
        for q in range(nq):
            xs[m, 0, q] = chip_sum(m, q, 2).astype(BF16)
        one = remote(("x1r", m), xs.at[m, 0, pl.ds(0, nq), pl.ds(0, te)], xr1.at[m, 0, pl.ds(0, nq)], right)
        two = remote(("x1l", m), xs.at[m, 0, pl.ds(0, nq), pl.ds(te, te)], xr1.at[m, 1, pl.ds(0, nq)], left)
        return send(one), send(two)

    def x_second(m, nq, first):
        result = []
        for side, (copy, r, to) in enumerate(((first[0], 1, right), (first[1], 3, left))):
            copy.wait_recv()
            lo = te * side
            for q in range(nq):
                total = chip_sum(m, q, r)
                xs[m, 1 + side, q] = total.astype(BF16)
                part = total[lo : lo + te] + xr1[m, side, q].astype(F32)
                xs[m, 1 + side, q, lo : lo + te] = part.astype(BF16)
            copy = remote(
                ("x2", m, side), xs.at[m, 1 + side, pl.ds(0, nq)], xr2.at[m, side, pl.ds(0, nq)], to
            )
            result.append(send(copy))
        return result

    def x_last(m, nq, second):
        for copy in second:
            copy.wait_recv()
        for q in range(nq):
            xsum[m, q] = chip_sum(m, q, 0) + xr2[m, 0, q].astype(F32) + xr2[m, 1, q].astype(F32)


    last = []

    def shard_of(ref, m):
        return ref.at[m, core, cols(tq * x, tq), cols(fourth * zc, fourth)]

    def ring_gather(name, m, block):
        own = block(tq * x, tq)
        to_right = send(remote((name, "1r", m), own, own, right))
        to_left = send(remote((name, "1l", m), own, own, left))
        copies = [send(remote((name, "c0", m), own, own, mate))]
        yield
        to_right.wait_recv()
        piece = block(tq * of4(x - 1), te)
        on_right = send(remote((name, "2r", m), piece, piece, right))
        to_left.wait_recv()
        piece = block(tq * of4(x + 1) + te, te)
        on_left = send(remote((name, "2l", m), piece, piece, left))
        for i in (1, 3):
            piece = block(tq * of4(x + i), tq)
            copies.append(send(remote((name, "c", i, m), piece, piece, mate)))
        yield
        on_right.wait_recv()
        on_left.wait_recv()
        piece = block(tq * of4(x + 2), tq)
        copies.append(send(remote((name, "c2", m), piece, piece, mate)))
        yield copies

    def spread(m):
        first = send(remote(("oz", m), shard_of(ob, m), shard_of(ob, m), zmate))
        yield
        first.wait_recv()
        for copies in ring_gather("o", m, lambda start, size: ob.at[m, core, cols(start, size)]):
            if copies is None:
                yield
        mine = local(("om", m), ob.at[m, core], out.at[(0, *span(m), cols(half * core, half))])
        mine.start()
        last.append(mine)
        yield
        for copy in copies:
            copy.wait_recv()
        other = local(("oo", m), ob.at[m, 1 - core], out.at[(0, *span(m), cols(half * (1 - core), half))])
        other.start()
        last.append(other)

    def interleave(chain, start):
        steps = [chain(m) for m in range(chunks)]
        turn = 0
        alive = set(range(chunks))
        while alive:
            for m in sorted(alive):
                if turn >= start[m] and next(steps[m], alive) is alive:
                    alive.discard(m)
            turn += 1
        for copy in last:
            copy.wait()
        for copy in started:
            copy.wait_send()
        last.clear()
        started.clear()


    def down_chain(m):
        g_loads[m].wait()
        for k in range(2):
            glow[m, 0, k] = gbuf[m, :, k * half : (k + 1) * half].astype(BF16)

        def partial(r):
            if m == 0:
                v_loads[(2, 1, 3, 0).index(r)].wait()
            rows = cols(fourth * of4(w + r), fourth)
            pa[m, r] = dot_nt(glow[m, 0, 0], v_raw[rows, :half]) + dot_nt(glow[m, 0, 1], v_raw[rows, half:])

        partial(2)
        one = send(remote(("a1u", m), pa.at[m, 2, pl.ds(0, th)], r1.at[m, 0], up))
        two = send(remote(("a1d", m), pa.at[m, 2, pl.ds(th, th)], r1.at[m, 1], down))
        partial(1)
        partial(3)
        yield
        one.wait_recv()
        pa[m, 1, :th] += r1[m, 0]
        three = send(remote(("a2u", m), pa.at[m, 1], r2.at[m, 0], up))
        two.wait_recv()
        pa[m, 3, th:] += r1[m, 1]
        four = send(remote(("a2d", m), pa.at[m, 3], r2.at[m, 1], down))
        partial(0)
        pre_down[m].wait()
        slope_stage(m, fourth)
        yield
        three.wait_recv()
        four.wait_recv()
        mine = cols(fourth * w, fourth)
        total = pa[m, 0] + r2[m, 0] + r2[m, 1]
        hid[m, :, mine] = (total * prev[m, :, :fourth]).astype(BF16)
        own = hid.at[m, :, mine]
        to_up = send(remote(("h1u", m), own, own, up))
        to_down = send(remote(("h1d", m), own, own, down))
        yield
        to_up.wait_recv()
        piece = hid.at[m, pl.ds(0, th), cols(fourth * of4(w - 1), fourth)]
        on_up = send(remote(("h2u", m), piece, piece, up))
        to_down.wait_recv()
        piece = hid.at[m, pl.ds(th, th), cols(fourth * of4(w + 1), fourth)]
        on_down = send(remote(("h2d", m), piece, piece, down))
        yield
        on_up.wait_recv()
        on_down.wait_recv()
        if m == 0:
            w_load.wait()

        def product(k):
            @pl.loop(0, 3)
            def _(n):
                rows = cols(half * k + (half // 3) * n, half // 3)
                pb[m, 0, k, :, cols((half // 3) * n, half // 3)] = dot_nt(hid[m], w_raw[rows, :])

        product(1 - core)
        copy = core_send(m, 0)
        product(core)
        yield
        copy.wait_recv()
        first = x_first(m, 1)
        yield
        second = x_second(m, 1, first)
        yield
        x_last(m, 1, second)
        columns = cols(fourth * zc, fourth)
        copy = send(remote(("z", m), xsum.at[m, 0, :, cols(fourth * (1 - zc), fourth)], zr.at[m, 0], zmate))
        yield
        copy.wait_recv()
        rows = cols(tq * x, tq)
        total = xsum[m, 0, :, columns] + zr[m, 0]
        total = total + gbuf[m, rows, cols(half * core + fourth * zc, fourth)]
        ob[m, core, rows, columns] = total
        gs[m] = total.astype(BF16)
        send(cross_copy(m))
        for copy in beyond_copies(m):
            send(copy)
        yield from spread(m)

    def cross_copy(m):
        return remote(("cross", m), shard_of(ob, m), bs.at[m], cross)

    def beyond_copies(m):
        return [
            remote(("beyond", i, m), gs.at[m], glow.at[m, b, core, cols(tq * x, tq), cols(fourth * zl, fourth)], to)
            for i, to in enumerate(beyond)
        ]

    @pl.when(s == 0)
    def _():
        interleave(down_chain, START_DOWN)


    def up_weights():
        for load in v_loads:
            load.wait()

        @pl.loop(0, tile // 128)
        def _(i):
            columns = cols(128 * i, 128)
            stripe[:tile, :] = v_raw[:, columns].astype(F32)
            for q in range(2):
                v_nat[q, :, columns] = stripe[pl.ds(q, half, stride=2), :].astype(BF16)

        w_load.wait()

        @pl.loop(0, half // 128)
        def _(i):
            for q in range(2):
                stripe[pl.ds(q, tile, stride=2), :] = w_raw[:, cols(half * q + 128 * i, 128)].astype(F32)
            w_nat[:, cols(128 * i, 128)] = stripe[...].astype(BF16)

    def up_chain(m):
        cross_copy(m).wait_recv()
        for copy in beyond_copies(m):
            copy.wait_recv()
        rows, columns = cols(tq * x, tq), cols(fourth * zc, fourth)
        glow[m, b, core, rows, columns] = bs[m].astype(BF16)
        for copies in ring_gather("g", m, lambda start, size: glow.at[m, :, core, cols(start, size)]):
            yield
        for copy in copies:
            copy.wait_recv()
        for part in range(2):
            columns = pl.ds(fourth * part, fourth)
            total = None
            for q in range(2):
                for k in range(2):
                    term = dot_nt(glow[m, q, k], v_nat[q, columns, k * half : (k + 1) * half])
                    total = term if total is None else total + term
            pf[m, :, columns] = total
            sb[m, :, columns] = total.astype(BF16)
        one = send(remote(("p1u", m), sb.at[m, pl.ds(0, th)], rl.at[m, 0], up))
        two = send(remote(("p1d", m), sb.at[m, pl.ds(th, th)], rl.at[m, 1], down))
        yield
        one.wait_recv()
        three = send(remote(("p2u", m), rl.at[m, 0], rp.at[m, pl.ds(0, th)], up))
        two.wait_recv()
        four = send(remote(("p2d", m), rl.at[m, 1], rp.at[m, pl.ds(th, th)], down))
        yield
        three.wait_recv()
        four.wait_recv()
        hid[m, :, :half] = ((pf[m] + rp[m].astype(F32)) * prev[m]).astype(BF16)

        def product(q, k):
            @pl.loop(0, 3)
            def _(n):
                rows = cols(tile * q + half * k + (half // 3) * n, half // 3)
                pb[m, q, k, :, cols((half // 3) * n, half // 3)] = dot_nt(hid[m, :, :half], w_nat[rows, :])

        copies = []
        for q in range(2):
            product(q, 1 - core)
            copies.append(core_send(m, q))
        for q in range(2):
            product(q, core)
        yield
        for copy in copies:
            copy.wait_recv()
        first = x_first(m, 2)
        yield
        second = x_second(m, 2, first)
        yield
        x_last(m, 2, second)
        copies = []
        for i, (to, q, zz) in enumerate(((corner, 1 - b, 1 - zc), (wmate, 1 - b, zc), (zmate, b, 1 - zc))):
            part = xsum.at[m, q, :, cols(fourth * zz, fourth)]
            copies.append(send(remote(("z", i, m), part, zr.at[m, i], to)))
        yield
        rows, columns = cols(tq * x, tq), cols(fourth * zc, fourth)
        total = xsum[m, b, :, columns]
        for i, copy in enumerate(copies):
            copy.wait_recv()
            total = total + zr[m, i]
        ob[m, core, rows, columns] = total + bs[m]
        yield from spread(m)

    @pl.when(s == 1)
    def _():
        up_weights()
        for m in range(chunks):
            pre_up[m].wait()
            slope_stage(m, half)
        interleave(up_chain, START_UP)


def local(grad_out, weight_in, weight_out, pre_act):
    batches, tok, tile = grad_out.shape
    chunks, whole, tok = batches * SPLIT, tok, tok // SPLIT
    half, fourth = tile // 2, tile // 4
    th, tq = tok // 2, tok // 4
    vmem = pltpu.VMEM
    scratch = [
        vmem((tile, tile), BF16),
        vmem((tile, tile), BF16),
        vmem((2, half, tile), BF16),
        vmem((2 * tile, half), BF16),
        vmem((2 * tile, 128), F32),
        vmem((chunks, tok, tile), F32),
        vmem((chunks, 2, 2, tok, half), BF16),
        vmem((chunks, tq, fourth), BF16),
        vmem((chunks, tok, half), F32),
        vmem((chunks, 4, tok, fourth), F32),
        vmem((chunks, 2, th, fourth), F32),
        vmem((chunks, 2, tok, fourth), F32),
        vmem((chunks, tok, tile), BF16),
        vmem((chunks, tok, half), F32),
        vmem((chunks, tok, half), BF16),
        vmem((chunks, 2, th, half), BF16),
        vmem((chunks, tok, half), BF16),
        vmem((chunks, 2, 2, tok, half), F32),
        vmem((chunks, 2, tok, half), F32),
        vmem((chunks, 3, 2, tq, half), BF16),
        vmem((chunks, 2, 2, tq // 2, half), BF16),
        vmem((chunks, 2, 2, tq, half), BF16),
        vmem((chunks, 2, tq, half), F32),
        vmem((chunks, 3, tq, fourth), F32),
        vmem((chunks, tq, fourth), F32),
        vmem((chunks, 2, tok, half), F32),
        pltpu.SemaphoreType.DMA((N_REMOTE,)),
        pltpu.SemaphoreType.DMA((N_REMOTE,)),
        pltpu.SemaphoreType.DMA((N_LOCAL,)),
    ]
    anywhere = pl.BlockSpec(memory_space=pl.ANY)
    return pl.pallas_call(
        kernel,
        out_shape=jax.ShapeDtypeStruct((1, batches, whole, tile), F32),
        in_specs=[anywhere] * 4,
        out_specs=anywhere,
        scratch_shapes=scratch,
        compiler_params=pltpu.CompilerParams(
            collective_id=0, has_side_effects=True, vmem_limit_bytes=67_000_000
        ),
    )(grad_out, weight_in, weight_out, pre_act)


def solution(mesh):
    return jax.shard_map(
        local,
        mesh=mesh,
        in_specs=(
            P(None, None, "wid"),
            P("section", "wid", "hid"),
            P("section", "hid", "wid"),
            P("section", None, None, "hid"),
        ),
        out_specs=P("section", None, None, "wid"),
        check_vma=False,
    )
```

```python
import jax
import jax.numpy as jnp
from jax import lax
from jax.experimental import pallas as pl
from jax.experimental.pallas import tpu as pltpu
from jax.sharding import PartitionSpec as P

F32 = jnp.float32
BF16 = jnp.bfloat16
MESH = pl.DeviceIdType.MESH
N_REMOTE = 272
N_LOCAL = 32
SPLIT = 2
START_DOWN = (0, 1, 2, 3)
START_UP = (0, 1, 2, 3)
NT = (((1,), (1,)), ((), ()))


def gelu_slope(pre):
    normal_cdf = 0.5 * (1.0 + lax.erf(pre * 0.7071067811865476))
    density = jnp.exp(-0.5 * pre * pre) * 0.3989422804014327
    return normal_cdf + pre * density


def dot_nn(a, b):
    return lax.dot_general(a, b, (((1,), (0,)), ((), ())), preferred_element_type=F32)


def dot_nt(a, b):
    return lax.dot_general(a, b, NT, preferred_element_type=F32)


def kernel(
    grad, win, wout, pre, out,
    v_raw, w_raw, vt, wt, stripe, gbuf, glow, gs, prev, pa, r1, r2, hid, pf, sb, rl, rp, pb, rc,
    xs, xr1, xr2, xsum, zr, ds, bs, ob,
    send_sem, recv_sem, local_sem,
):
    s = lax.axis_index("section")
    h = lax.axis_index("hid")
    w = lax.axis_index("wid")
    x = lax.div(h, 4)
    zl = lax.rem(lax.div(h, 2), 2)
    core = lax.rem(h, 2)
    c = lax.div(w, 2)
    b = lax.rem(w, 2)
    zc = zl + s - 2 * zl * s
    tile = grad.shape[2]
    chunks, tok = pb.shape[0], pb.shape[3]
    half, fourth = tile // 2, tile // 4
    th, tq = tok // 2, tok // 4
    te = tq // 2

    def device(dx=0, dw=0, flip_core=False, flip_z=False, flip_s=False, flip_w=False):
        nx = lax.rem(x + dx + 4, 4) if dx else x
        nz = 1 - zl if flip_z else zl
        nc = 1 - core if flip_core else core
        nw = lax.rem(w + dw + 4, 4) if dw else w
        if flip_w:
            nw = w + 1 - 2 * b
        return {"section": 1 - s if flip_s else s, "hid": nx * 4 + nz * 2 + nc, "wid": nw}

    right, left = device(dx=1), device(dx=-1)
    up, down = device(dw=1), device(dw=-1)
    mate = device(flip_core=True)
    zmate = device(flip_z=True)
    wmate = device(flip_w=True)
    corner = device(flip_w=True, flip_z=True)
    cross = device(flip_s=True, flip_z=True)
    beyond = [
        cross, device(flip_s=True), device(flip_s=True, flip_z=True, flip_w=True), device(flip_s=True, flip_w=True)
    ]

    keys = {}

    def remote(key, src, dst, to):
        index = keys.setdefault(key, len(keys))
        return pltpu.make_async_remote_copy(
            src_ref=src, dst_ref=dst, send_sem=send_sem.at[index], recv_sem=recv_sem.at[index],
            device_id=to, device_id_type=MESH,
        )

    local_keys = {}

    def local(key, src, dst):
        index = local_keys.setdefault(key, len(local_keys))
        return pltpu.make_async_copy(src, dst, local_sem.at[index])

    def of4(i):
        return lax.rem(i + 4, 4)

    def cols(start, size):
        return pl.ds(pl.multiple_of(start, size), size)

    started = []

    def send(copy):
        copy.start()
        started.append(copy)
        return copy


    def span(m):
        return m // SPLIT, pl.ds(tok * (m % SPLIT), tok)

    pre_down = [
        local(("pre", m), pre.at[(0, *span(m), cols(fourth * w, fourth))], prev.at[m, :, pl.ds(0, fourth)])
        for m in range(chunks)
    ]
    pre_up = [
        local(("pre", m), pre.at[(0, *span(m), cols(half * b, half))], prev.at[m]) for m in range(chunks)
    ]
    v_loads = [
        local(("v", r), wout.at[0, cols(fourth * of4(w + r), fourth), :],
              v_raw.at[cols(fourth * of4(w + r), fourth), :])
        for r in (2, 1, 3, 0)
    ]
    w_load = local("w", win.at[0], w_raw)
    g_loads = [local(("g", m), grad.at[span(m)], gbuf.at[m]) for m in range(chunks)]

    @pl.when(s == 0)
    def _():
        g_loads[0].start()

    for load in v_loads:
        load.start()
    w_load.start()

    @pl.when(s == 0)
    def _():
        for load in (*pre_down, *g_loads[1:]):
            load.start()

    @pl.when(s == 1)
    def _():
        for load in pre_up:
            load.start()

    barrier = pltpu.get_barrier_semaphore()
    peers = [right, left, up, down, mate, zmate, corner, *beyond]
    for peer in peers:
        pl.semaphore_signal(barrier, inc=1, device_id=peer, device_id_type=MESH)

    def all_in():
        pl.semaphore_wait(barrier, len(peers))

    def slope_stage(m, width):
        @pl.loop(0, 4)
        def _(i):
            rows = cols(i * (tok // 4), tok // 4)
            prev[m, rows, :width] = gelu_slope(prev[m, rows, :width])


    def core_send(m, q):
        return send(remote(("core", m, q), pb.at[m, q, 1 - core], rc.at[m, q], mate))

    def x_rows(r):
        return cols(tq * of4(x + r), tq)

    def chip_sum(m, q, r):
        rows = x_rows(r)
        return pb[m, q, core, rows, :] + rc[m, q, rows, :]

    def x_first(m, nq):
        for q in range(nq):
            xs[m, 0, q] = chip_sum(m, q, 2).astype(BF16)
        one = remote(("x1r", m), xs.at[m, 0, pl.ds(0, nq), pl.ds(0, te)], xr1.at[m, 0, pl.ds(0, nq)], right)
        two = remote(("x1l", m), xs.at[m, 0, pl.ds(0, nq), pl.ds(te, te)], xr1.at[m, 1, pl.ds(0, nq)], left)
        return send(one), send(two)

    def x_second(m, nq, first):
        result = []
        for side, (copy, r, to) in enumerate(((first[0], 1, right), (first[1], 3, left))):
            copy.wait_recv()
            lo = te * side
            for q in range(nq):
                total = chip_sum(m, q, r)
                xs[m, 1 + side, q] = total.astype(BF16)
                part = total[lo : lo + te] + xr1[m, side, q].astype(F32)
                xs[m, 1 + side, q, lo : lo + te] = part.astype(BF16)
            copy = remote(
                ("x2", m, side), xs.at[m, 1 + side, pl.ds(0, nq)], xr2.at[m, side, pl.ds(0, nq)], to
            )
            result.append(send(copy))
        return result

    def x_last(m, nq, second):
        for copy in second:
            copy.wait_recv()
        for q in range(nq):
            xsum[m, q] = chip_sum(m, q, 0) + xr2[m, 0, q].astype(F32) + xr2[m, 1, q].astype(F32)


    last = []

    def shard_of(ref, m):
        return ref.at[m, core, cols(tq * x, tq), cols(fourth * zc, fourth)]

    def ring_gather(name, m, block):
        own = block(tq * x, tq)
        to_right = send(remote((name, "1r", m), own, own, right))
        to_left = send(remote((name, "1l", m), own, own, left))
        copies = [send(remote((name, "c0", m), own, own, mate))]
        yield
        to_right.wait_recv()
        piece = block(tq * of4(x - 1), te)
        on_right = send(remote((name, "2r", m), piece, piece, right))
        to_left.wait_recv()
        piece = block(tq * of4(x + 1) + te, te)
        on_left = send(remote((name, "2l", m), piece, piece, left))
        for i in (1, 3):
            piece = block(tq * of4(x + i), tq)
            copies.append(send(remote((name, "c", i, m), piece, piece, mate)))
        yield
        on_right.wait_recv()
        on_left.wait_recv()
        piece = block(tq * of4(x + 2), tq)
        copies.append(send(remote((name, "c2", m), piece, piece, mate)))
        yield copies

    def spread(m):
        first = send(remote(("oz", m), shard_of(ob, m), shard_of(ob, m), zmate))
        yield
        first.wait_recv()
        for copies in ring_gather("o", m, lambda start, size: ob.at[m, core, cols(start, size)]):
            if copies is None:
                yield
        mine = local(("om", m), ob.at[m, core], out.at[(0, *span(m), cols(half * core, half))])
        mine.start()
        last.append(mine)
        yield
        for copy in copies:
            copy.wait_recv()
        other = local(("oo", m), ob.at[m, 1 - core], out.at[(0, *span(m), cols(half * (1 - core), half))])
        other.start()
        last.append(other)

    def interleave(chain, start):
        steps = [chain(m) for m in range(chunks)]
        turn = 0
        alive = set(range(chunks))
        while alive:
            for m in sorted(alive):
                if turn >= start[m] and next(steps[m], alive) is alive:
                    alive.discard(m)
            turn += 1
        for copy in last:
            copy.wait()
        for copy in started:
            copy.wait_send()
        last.clear()
        started.clear()


    def down_chain(m):
        g_loads[m].wait()
        for k in range(2):
            glow[m, 0, k] = gbuf[m, :, k * half : (k + 1) * half].astype(BF16)

        def partial(r):
            if m == 0:
                v_loads[(2, 1, 3, 0).index(r)].wait()
            rows = cols(fourth * of4(w + r), fourth)
            pa[m, r] = dot_nt(glow[m, 0, 0], v_raw[rows, :half]) + dot_nt(glow[m, 0, 1], v_raw[rows, half:])

        partial(2)
        if m == 0:
            all_in()
        one = send(remote(("a1u", m), pa.at[m, 2, pl.ds(0, th)], r1.at[m, 0], up))
        two = send(remote(("a1d", m), pa.at[m, 2, pl.ds(th, th)], r1.at[m, 1], down))
        partial(1)
        partial(3)
        yield
        one.wait_recv()
        pa[m, 1, :th] += r1[m, 0]
        three = send(remote(("a2u", m), pa.at[m, 1], r2.at[m, 0], up))
        two.wait_recv()
        pa[m, 3, th:] += r1[m, 1]
        four = send(remote(("a2d", m), pa.at[m, 3], r2.at[m, 1], down))
        partial(0)
        pre_down[m].wait()
        slope_stage(m, fourth)
        yield
        three.wait_recv()
        four.wait_recv()
        mine = cols(fourth * w, fourth)
        total = pa[m, 0] + r2[m, 0] + r2[m, 1]
        hid[m, :, mine] = (total * prev[m, :, :fourth]).astype(BF16)
        own = hid.at[m, :, mine]
        to_up = send(remote(("h1u", m), own, own, up))
        to_down = send(remote(("h1d", m), own, own, down))
        yield
        to_up.wait_recv()
        piece = hid.at[m, pl.ds(0, th), cols(fourth * of4(w - 1), fourth)]
        on_up = send(remote(("h2u", m), piece, piece, up))
        to_down.wait_recv()
        piece = hid.at[m, pl.ds(th, th), cols(fourth * of4(w + 1), fourth)]
        on_down = send(remote(("h2d", m), piece, piece, down))
        yield
        on_up.wait_recv()
        on_down.wait_recv()
        if m == 0:
            w_load.wait()

        def product(k):
            pb[m, 0, k] = dot_nt(hid[m], w_raw[cols(half * k, half), :])

        product(1 - core)
        copy = core_send(m, 0)
        product(core)
        yield
        copy.wait_recv()
        first = x_first(m, 1)
        yield
        second = x_second(m, 1, first)
        yield
        x_last(m, 1, second)
        columns = cols(fourth * zc, fourth)
        copy = send(remote(("z", m), xsum.at[m, 0, :, cols(fourth * (1 - zc), fourth)], zr.at[m, 0], zmate))
        yield
        copy.wait_recv()
        rows = cols(tq * x, tq)
        total = xsum[m, 0, :, columns] + zr[m, 0]
        ds[m] = total
        ob[m, core, rows, columns] = total.astype(BF16)
        gs[m] = (total + gbuf[m, rows, cols(half * core + fourth * zc, fourth)]).astype(BF16)
        for copy in beyond_copies(m):
            send(copy)
        send(cross_copy(m))
        yield from spread(m)

    def cross_copy(m):
        return remote(("cross", m), ds.at[m], bs.at[m], cross)

    def beyond_copies(m):
        return [
            remote(("beyond", i, m), gs.at[m], glow.at[m, b, core, cols(tq * x, tq), cols(fourth * zl, fourth)], to)
            for i, to in enumerate(beyond)
        ]

    @pl.when(s == 0)
    def _():
        interleave(down_chain, START_DOWN)


    def up_weights():
        for load in v_loads:
            load.wait()

        @pl.loop(0, tile // 128)
        def _(i):
            columns = cols(128 * i, 128)
            stripe[:tile, :] = v_raw[:, columns].astype(F32)
            for q in range(2):
                vt[q, columns, :] = stripe[pl.ds(q, half, stride=2), :].T.astype(BF16)

        w_load.wait()

        @pl.loop(0, half // 128)
        def _(i):
            for q in range(2):
                stripe[pl.ds(q, tile, stride=2), :] = w_raw[:, cols(half * q + 128 * i, 128)].astype(F32)
            wt[cols(128 * i, 128), :] = stripe[...].T.astype(BF16)

    def up_chain(m):
        for copy in beyond_copies(m):
            copy.wait_recv()
        for copies in ring_gather("g", m, lambda start, size: glow.at[m, :, core, cols(start, size)]):
            yield
        for copy in copies:
            copy.wait_recv()
        swaps = []
        for part in range(2):
            columns = pl.ds(fourth * part, fourth)
            total = None
            for q in range(2):
                for k in range(2):
                    term = dot_nn(glow[m, q, k], vt[q, k * half : (k + 1) * half, columns])
                    total = term if total is None else total + term
            pf[m, :, columns] = total
            sb[m, part] = total.astype(BF16)
            one = remote(("p1u", m, part), sb.at[m, part, pl.ds(0, th)], rl.at[m, part, 0], up)
            two = remote(("p1d", m, part), sb.at[m, part, pl.ds(th, th)], rl.at[m, part, 1], down)
            swaps.append((send(one), send(two)))
        yield
        relayed = []
        for part, (one, two) in enumerate(swaps):
            one.wait_recv()
            three = remote(("p2u", m, part), rl.at[m, part, 0], rp.at[m, part, pl.ds(0, th)], up)
            relayed.append(send(three))
            two.wait_recv()
            four = remote(("p2d", m, part), rl.at[m, part, 1], rp.at[m, part, pl.ds(th, th)], down)
            relayed.append(send(four))
        yield
        for copy in relayed:
            copy.wait_recv()
        for part in range(2):
            columns = pl.ds(fourth * part, fourth)
            total = pf[m, :, columns] + rp[m, part].astype(F32)
            hid[m, :, columns] = (total * prev[m, :, columns]).astype(BF16)

        def product(q, k):
            pb[m, q, k] = dot_nn(hid[m, :, :half], wt[:, cols(tile * q + half * k, half)])

        copies = []
        for q in range(2):
            product(q, 1 - core)
            copies.append(core_send(m, q))
        for q in range(2):
            product(q, core)
        yield
        for copy in copies:
            copy.wait_recv()
        first = x_first(m, 2)
        yield
        second = x_second(m, 2, first)
        yield
        x_last(m, 2, second)
        copies = []
        for i, (to, q, zz) in enumerate(((corner, 1 - b, 1 - zc), (wmate, 1 - b, zc), (zmate, b, 1 - zc))):
            part = xsum.at[m, q, :, cols(fourth * zz, fourth)]
            copies.append(send(remote(("z", i, m), part, zr.at[m, i], to)))
        yield
        rows, columns = cols(tq * x, tq), cols(fourth * zc, fourth)
        total = xsum[m, b, :, columns]
        for i, copy in enumerate(copies):
            copy.wait_recv()
            total = total + zr[m, i]
        cross_copy(m).wait_recv()
        ob[m, core, rows, columns] = (total + bs[m]).astype(BF16)
        yield from spread(m)

    @pl.when(s == 1)
    def _():
        up_weights()
        all_in()
        for m in range(chunks):
            pre_up[m].wait()
            slope_stage(m, half)
        interleave(up_chain, START_UP)


def local(grad_out, weight_in, weight_out, pre_act):
    batches, tok, tile = grad_out.shape
    chunks, whole, tok = batches * SPLIT, tok, tok // SPLIT
    half, fourth = tile // 2, tile // 4
    th, tq = tok // 2, tok // 4
    vmem = pltpu.VMEM
    scratch = [
        vmem((tile, tile), BF16),
        vmem((tile, tile), BF16),
        vmem((2, tile, half), BF16),
        vmem((half, 2 * tile), BF16),
        vmem((2 * tile, 128), F32),
        vmem((chunks, tok, tile), F32),
        vmem((chunks, 2, 2, tok, half), BF16),
        vmem((chunks, tq, fourth), BF16),
        vmem((chunks, tok, half), F32),
        vmem((chunks, 4, tok, fourth), F32),
        vmem((chunks, 2, th, fourth), F32),
        vmem((chunks, 2, tok, fourth), F32),
        vmem((chunks, tok, tile), BF16),
        vmem((chunks, tok, half), F32),
        vmem((chunks, 2, tok, fourth), BF16),
        vmem((chunks, 2, 2, th, fourth), BF16),
        vmem((chunks, 2, tok, fourth), BF16),
        vmem((chunks, 2, 2, tok, half), F32),
        vmem((chunks, 2, tok, half), F32),
        vmem((chunks, 3, 2, tq, half), BF16),
        vmem((chunks, 2, 2, tq // 2, half), BF16),
        vmem((chunks, 2, 2, tq, half), BF16),
        vmem((chunks, 2, tq, half), F32),
        vmem((chunks, 3, tq, fourth), F32),
        vmem((chunks, tq, fourth), F32),
        vmem((chunks, tq, fourth), F32),
        vmem((chunks, 2, tok, half), BF16),
        pltpu.SemaphoreType.DMA((N_REMOTE,)),
        pltpu.SemaphoreType.DMA((N_REMOTE,)),
        pltpu.SemaphoreType.DMA((N_LOCAL,)),
    ]
    anywhere = pl.BlockSpec(memory_space=pl.ANY)
    change = pl.pallas_call(
        kernel,
        out_shape=jax.ShapeDtypeStruct((1, batches, whole, tile), BF16),
        in_specs=[anywhere] * 4,
        out_specs=anywhere,
        scratch_shapes=scratch,
        compiler_params=pltpu.CompilerParams(
            collective_id=0, has_side_effects=True, vmem_limit_bytes=67_000_000
        ),
    )(grad_out, weight_in, weight_out, pre_act)
    return grad_out[None] + change.astype(F32)


def solution(mesh):
    return jax.shard_map(
        local,
        mesh=mesh,
        in_specs=(
            P(None, None, "wid"),
            P("section", "wid", "hid"),
            P("section", "hid", "wid"),
            P("section", None, None, "hid"),
        ),
        out_specs=P("section", None, None, "wid"),
        check_vma=False,
    )
```

```python
import functools

import jax
import jax.numpy as jnp
from jax import lax
from jax.experimental import pallas as pl
from jax.experimental.pallas import tpu as pltpu
from jax.sharding import PartitionSpec as P

F32 = jnp.float32
BF16 = jnp.bfloat16
MESH = pl.DeviceIdType.MESH
N_REMOTE = 272
N_LOCAL = 32
SPLIT = 2
START_DOWN = (0, 1, 2, 3)
START_UP = (0, 1, 2, 3)
NT = (((1,), (1,)), ((), ()))


def gelu_slope(pre):
    normal_cdf = 0.5 * (1.0 + lax.erf(pre * 0.7071067811865476))
    density = jnp.exp(-0.5 * pre * pre) * 0.3989422804014327
    return normal_cdf + pre * density


def pack(ref, value):
    rows, columns = value.shape
    blocks = [value[:, i : i + 128] for i in range(0, columns, 128)]
    top = functools.reduce(jnp.maximum, [jnp.max(jnp.abs(block), axis=0, keepdims=True) for block in blocks])
    scale = (80.0 / jnp.maximum(top, 1e-30)).astype(BF16)
    for i, block in enumerate(blocks):
        ref[rows * i : rows * (i + 1), :] = jnp.exp(block * scale.astype(F32)).astype(BF16)
    ref[rows * len(blocks) :, :] = jnp.broadcast_to(scale.astype(F32), (16, 128)).astype(BF16)


def unpack(ref, rows, columns):
    count = columns // 128
    step = 1.0 / ref[rows * count :, :].astype(F32)[:1]
    return jnp.concatenate(
        [jnp.log(ref[rows * i : rows * (i + 1), :].astype(F32)) * step for i in range(count)], axis=1
    )


def dot_nn(a, b):
    return lax.dot_general(a, b, (((1,), (0,)), ((), ())), preferred_element_type=F32)


def dot_nt(a, b):
    return lax.dot_general(a, b, NT, preferred_element_type=F32)


def kernel(
    grad, win, wout, pre, out,
    v_raw, w_raw, vt, wt, stripe, gbuf, gd, glow, gs, prev, pa, a1, a2, r1, r2, hid, pf, sb, rl, rp, pb, rc,
    xs, xr1, xr2, xsum, zs, zr, ds, bs, ob,
    send_sem, recv_sem, local_sem,
):
    s = lax.axis_index("section")
    h = lax.axis_index("hid")
    w = lax.axis_index("wid")
    x = lax.div(h, 4)
    zl = lax.rem(lax.div(h, 2), 2)
    core = lax.rem(h, 2)
    c = lax.div(w, 2)
    b = lax.rem(w, 2)
    tile = grad.shape[2]
    chunks, tok = pb.shape[0], pb.shape[3]
    half, fourth = tile // 2, tile // 4
    th, tq = tok // 2, tok // 4
    te = tq // 2

    def device(dx=0, dw=0, flip_core=False, flip_z=False, flip_s=False, flip_w=False):
        nx = lax.rem(x + dx + 4, 4) if dx else x
        nz = 1 - zl if flip_z else zl
        nc = 1 - core if flip_core else core
        nw = lax.rem(w + dw + 4, 4) if dw else w
        if flip_w:
            nw = w + 1 - 2 * b
        return {"section": 1 - s if flip_s else s, "hid": nx * 4 + nz * 2 + nc, "wid": nw}

    right, left = device(dx=1), device(dx=-1)
    up, down = device(dw=1), device(dw=-1)
    mate = device(flip_core=True)
    zmate = device(flip_z=True)
    wmate = device(flip_w=True)
    corner = device(flip_w=True, flip_z=True)
    cross = device(flip_s=True, flip_z=True)
    beyond = [cross, device(flip_s=True, flip_z=True, flip_w=True)]

    keys = {}

    def remote(key, src, dst, to):
        index = keys.setdefault(key, len(keys))
        return pltpu.make_async_remote_copy(
            src_ref=src, dst_ref=dst, send_sem=send_sem.at[index], recv_sem=recv_sem.at[index],
            device_id=to, device_id_type=MESH,
        )

    local_keys = {}

    def local(key, src, dst):
        index = local_keys.setdefault(key, len(local_keys))
        return pltpu.make_async_copy(src, dst, local_sem.at[index])

    def of4(i):
        return lax.rem(i + 4, 4)

    def cols(start, size):
        return pl.ds(pl.multiple_of(start, size), size)

    started = []

    def send(copy):
        copy.start()
        started.append(copy)
        return copy


    def span(m):
        return m // SPLIT, pl.ds(tok * (m % SPLIT), tok)

    pre_down = [
        local(("pre", m), pre.at[(0, *span(m), cols(fourth * w, fourth))], prev.at[m, :, pl.ds(0, fourth)])
        for m in range(chunks)
    ]
    pre_up = [
        local(("pre", m), pre.at[(0, *span(m), cols(half * b, half))], prev.at[m]) for m in range(chunks)
    ]
    v_loads = [
        local(("v", r), wout.at[0, cols(fourth * of4(w + r), fourth), :],
              v_raw.at[cols(fourth * of4(w + r), fourth), :])
        for r in (2, 1, 3, 0)
    ]
    w_load = local("w", win.at[0], w_raw)
    g_loads = [local(("g", m), grad.at[m], gbuf.at[m]) for m in range(chunks // SPLIT)]

    @pl.when(s == 0)
    def _():
        g_loads[0].start()

    for load in v_loads:
        load.start()
    w_load.start()

    @pl.when(s == 0)
    def _():
        for load in (*pre_down, *g_loads[1:]):
            load.start()

    @pl.when(s == 1)
    def _():
        for load in pre_up:
            load.start()

    barrier = pltpu.get_barrier_semaphore()
    peers = [right, left, up, down, mate, zmate, corner, *beyond]
    for peer in peers:
        pl.semaphore_signal(barrier, inc=1, device_id=peer, device_id_type=MESH)

    def all_in():
        pl.semaphore_wait(barrier, len(peers))

    def slope_stage(m, width):
        @pl.loop(0, 4)
        def _(i):
            rows = cols(i * (tok // 4), tok // 4)
            prev[m, rows, :width] = gelu_slope(prev[m, rows, :width])


    def core_send(m, q):
        return send(remote(("core", m, q), pb.at[m, q, 1 - core], rc.at[m, q], mate))

    def x_rows(r):
        return cols(tq * of4(x + r), tq)

    def chip_sum(m, q, r):
        rows = x_rows(r)
        return pb[m, q, core, rows, :] + rc[m, q, rows, :]

    def x_first(m, nq):
        for q in range(nq):
            xs[m, 0, q] = chip_sum(m, q, 2).astype(BF16)
        one = remote(("x1r", m), xs.at[m, 0, pl.ds(0, nq), pl.ds(0, te)], xr1.at[m, 0, pl.ds(0, nq)], right)
        two = remote(("x1l", m), xs.at[m, 0, pl.ds(0, nq), pl.ds(te, te)], xr1.at[m, 1, pl.ds(0, nq)], left)
        return send(one), send(two)

    def x_second(m, nq, first):
        result = []
        for side, (copy, r, to) in enumerate(((first[0], 1, right), (first[1], 3, left))):
            copy.wait_recv()
            lo = te * side
            for q in range(nq):
                total = chip_sum(m, q, r)
                xs[m, 1 + side, q] = total.astype(BF16)
                part = total[lo : lo + te] + xr1[m, side, q].astype(F32)
                xs[m, 1 + side, q, lo : lo + te] = part.astype(BF16)
            copy = remote(
                ("x2", m, side), xs.at[m, 1 + side, pl.ds(0, nq)], xr2.at[m, side, pl.ds(0, nq)], to
            )
            result.append(send(copy))
        return result

    def x_last(m, nq, second):
        for copy in second:
            copy.wait_recv()
        for q in range(nq):
            xsum[m, q] = chip_sum(m, q, 0) + xr2[m, 0, q].astype(F32) + xr2[m, 1, q].astype(F32)


    last = []

    def ring_gather(name, m, block):
        own = block(tq * x, tq)
        to_right = send(remote((name, "1r", m), own, own, right))
        to_left = send(remote((name, "1l", m), own, own, left))
        copies = [send(remote((name, "c0", m), own, own, mate))]
        yield
        to_right.wait_recv()
        piece = block(tq * of4(x - 1), te)
        on_right = send(remote((name, "2r", m), piece, piece, right))
        to_left.wait_recv()
        piece = block(tq * of4(x + 1) + te, te)
        on_left = send(remote((name, "2l", m), piece, piece, left))
        for i in (1, 3):
            piece = block(tq * of4(x + i), tq)
            copies.append(send(remote((name, "c", i, m), piece, piece, mate)))
        yield
        on_right.wait_recv()
        on_left.wait_recv()
        piece = block(tq * of4(x + 2), tq)
        copies.append(send(remote((name, "c2", m), piece, piece, mate)))
        yield copies

    def spread(m):
        for copies in ring_gather("o", m, lambda start, size: ob.at[m, core, cols(start, size)]):
            if copies is None:
                yield
        mine = local(("om", m), ob.at[m, core], out.at[(0, *span(m), cols(half * core, half))])
        mine.start()
        last.append(mine)
        yield
        for copy in copies:
            copy.wait_recv()
        other = local(("oo", m), ob.at[m, 1 - core], out.at[(0, *span(m), cols(half * (1 - core), half))])
        other.start()
        last.append(other)

    def interleave(chain, start):
        steps = [chain(m) for m in range(chunks)]
        turn = 0
        alive = set(range(chunks))
        while alive:
            for m in sorted(alive):
                if turn >= start[m] and next(steps[m], alive) is alive:
                    alive.discard(m)
            turn += 1
        for copy in last:
            copy.wait()
        for copy in started:
            copy.wait_send()
        last.clear()
        started.clear()


    def down_chain(m):
        batch, rows = m // SPLIT, pl.ds(tok * (m % SPLIT), tok)

        def partial(r):
            if m == 0:
                v_loads[(2, 1, 3, 0).index(r)].wait()
            units = cols(fourth * of4(w + r), fourth)
            pa[batch, r] = dot_nt(gd[batch, 0], v_raw[units, :half]) + dot_nt(gd[batch, 1], v_raw[units, half:])

        if m % SPLIT == 0:
            g_loads[batch].wait()
            for k in range(2):
                gd[batch, k] = gbuf[batch, :, k * half : (k + 1) * half].astype(BF16)
            partial(2)
        if m == 0:
            all_in()
        first = pa[batch, 2, rows]
        pack(a1.at[m, 0], first[:th])
        one = send(remote(("a1u", m), a1.at[m, 0], r1.at[m, 0], up))
        pack(a1.at[m, 1], first[th:])
        two = send(remote(("a1d", m), a1.at[m, 1], r1.at[m, 1], down))
        if m % SPLIT == 0:
            partial(1)
            partial(3)
        yield
        one.wait_recv()
        part = pa[batch, 1, rows]
        pack(a2.at[m, 0], jnp.concatenate([part[:th] + unpack(r1.at[m, 0], th, fourth), part[th:]], axis=0))
        three = send(remote(("a2u", m), a2.at[m, 0], r2.at[m, 0], up))
        two.wait_recv()
        part = pa[batch, 3, rows]
        pack(a2.at[m, 1], jnp.concatenate([part[:th], part[th:] + unpack(r1.at[m, 1], th, fourth)], axis=0))
        four = send(remote(("a2d", m), a2.at[m, 1], r2.at[m, 1], down))
        if m % SPLIT == 0:
            partial(0)
        pre_down[m].wait()
        slope_stage(m, fourth)
        yield
        three.wait_recv()
        four.wait_recv()
        mine = cols(fourth * w, fourth)
        total = pa[batch, 0, rows] + unpack(r2.at[m, 0], tok, fourth) + unpack(r2.at[m, 1], tok, fourth)
        hid[m, :, mine] = (total * prev[m, :, :fourth]).astype(BF16)
        own = hid.at[m, :, mine]
        to_up = send(remote(("h1u", m), own, own, up))
        to_down = send(remote(("h1d", m), own, own, down))
        yield
        to_up.wait_recv()
        piece = hid.at[m, pl.ds(0, th), cols(fourth * of4(w - 1), fourth)]
        on_up = send(remote(("h2u", m), piece, piece, up))
        to_down.wait_recv()
        piece = hid.at[m, pl.ds(th, th), cols(fourth * of4(w + 1), fourth)]
        on_down = send(remote(("h2d", m), piece, piece, down))
        yield
        on_up.wait_recv()
        on_down.wait_recv()
        if m == 0:
            w_load.wait()

        def product(k):
            pb[m, 0, k] = dot_nt(hid[m], w_raw[cols(half * k, half), :])

        product(1 - core)
        copy = core_send(m, 0)
        product(core)
        yield
        copy.wait_recv()
        first = x_first(m, 1)
        yield
        second = x_second(m, 1, first)
        yield
        x_last(m, 1, second)
        pack(zs.at[m, 0], xsum[m, 0])
        copy = send(remote(("z", 0, m), zs.at[m, 0], zr.at[m, 0], zmate))
        yield
        copy.wait_recv()
        rows = cols(tq * x, tq)
        total = unpack(zs.at[m, 0], tq, half) + unpack(zr.at[m, 0], tq, half)
        grad_rows = pl.ds(pl.multiple_of(tok * (m % SPLIT) + tq * x, tq), tq)
        gs[m] = (total + gbuf[m // SPLIT, grad_rows, cols(half * core, half)]).astype(BF16)
        for copy in beyond_copies(m):
            send(copy)
        pack(ds.at[m], total)
        send(cross_copy(m))
        ob[m, core, rows] = total.astype(BF16)
        yield from spread(m)

    def cross_copy(m):
        return remote(("cross", m), ds.at[m], bs.at[m], cross)

    def beyond_copies(m):
        return [
            remote(("beyond", i, m), gs.at[m], glow.at[m, b, core, cols(tq * x, tq)], to)
            for i, to in enumerate(beyond)
        ]

    @pl.when(s == 0)
    def _():
        interleave(down_chain, START_DOWN)


    def up_weights():
        for load in v_loads:
            load.wait()

        @pl.loop(0, tile // 128)
        def _(i):
            columns = cols(128 * i, 128)
            stripe[:tile, :] = v_raw[:, columns].astype(F32)
            for q in range(2):
                vt[q, columns, :] = stripe[pl.ds(q, half, stride=2), :].T.astype(BF16)

        w_load.wait()

        @pl.loop(0, half // 128)
        def _(i):
            for q in range(2):
                stripe[pl.ds(q, tile, stride=2), :] = w_raw[:, cols(half * q + 128 * i, 128)].astype(F32)
            wt[cols(128 * i, 128), :] = stripe[...].T.astype(BF16)

    def up_chain(m):
        for copy in beyond_copies(m):
            copy.wait_recv()
        for copies in ring_gather("g", m, lambda start, size: glow.at[m, :, core, cols(start, size)]):
            yield
        for copy in copies:
            copy.wait_recv()
        swaps = []
        for part in range(2):
            columns = pl.ds(fourth * part, fourth)
            total = None
            for q in range(2):
                for k in range(2):
                    term = dot_nn(glow[m, q, k], vt[q, k * half : (k + 1) * half, columns])
                    total = term if total is None else total + term
            pf[m, :, columns] = total
            sb[m, part] = total.astype(BF16)
            one = remote(("p1u", m, part), sb.at[m, part, pl.ds(0, th)], rl.at[m, part, 0], up)
            two = remote(("p1d", m, part), sb.at[m, part, pl.ds(th, th)], rl.at[m, part, 1], down)
            swaps.append((send(one), send(two)))
        yield
        relayed = []
        for part, (one, two) in enumerate(swaps):
            one.wait_recv()
            three = remote(("p2u", m, part), rl.at[m, part, 0], rp.at[m, part, pl.ds(0, th)], up)
            relayed.append(send(three))
            two.wait_recv()
            four = remote(("p2d", m, part), rl.at[m, part, 1], rp.at[m, part, pl.ds(th, th)], down)
            relayed.append(send(four))
        yield
        for copy in relayed:
            copy.wait_recv()
        for part in range(2):
            columns = pl.ds(fourth * part, fourth)
            total = pf[m, :, columns] + rp[m, part].astype(F32)
            hid[m, :, columns] = (total * prev[m, :, columns]).astype(BF16)

        def product(q, k):
            pb[m, q, k] = dot_nn(hid[m, :, :half], wt[:, cols(tile * q + half * k, half)])

        copies = []
        for q in range(2):
            product(q, 1 - core)
            copies.append(core_send(m, q))
        for q in range(2):
            product(q, core)
        yield
        for copy in copies:
            copy.wait_recv()
        first = x_first(m, 2)
        yield
        second = x_second(m, 2, first)
        yield
        x_last(m, 2, second)
        pack(zs.at[m, 1], xsum[m, 1 - b])
        copies = [send(remote(("z", i, m), zs.at[m, 1], zr.at[m, i], to)) for i, to in ((2, corner), (1, wmate))]
        pack(zs.at[m, 0], xsum[m, b])
        copies.append(send(remote(("z", 0, m), zs.at[m, 0], zr.at[m, 0], zmate)))
        yield
        for copy in copies:
            copy.wait_recv()
        cross_copy(m).wait_recv()
        terms = [unpack(part, tq, half) for part in (zs.at[m, 0], zr.at[m, 0], zr.at[m, 1], zr.at[m, 2])]
        total = (terms[0] + terms[1]) + (terms[2] + terms[3])
        ob[m, core, cols(tq * x, tq)] = (total + unpack(bs.at[m], tq, half)).astype(BF16)
        yield from spread(m)

    @pl.when(s == 1)
    def _():
        up_weights()
        all_in()
        for m in range(chunks):
            pre_up[m].wait()
            slope_stage(m, half)
        interleave(up_chain, START_UP)


def local(grad_out, weight_in, weight_out, pre_act):
    batches, tok, tile = grad_out.shape
    chunks, whole, tok = batches * SPLIT, tok, tok // SPLIT
    half, fourth = tile // 2, tile // 4
    th, tq = tok // 2, tok // 4
    vmem = pltpu.VMEM
    scratch = [
        vmem((tile, tile), BF16),
        vmem((tile, tile), BF16),
        vmem((2, tile, half), BF16),
        vmem((half, 2 * tile), BF16),
        vmem((2 * tile, 128), F32),
        vmem((batches, whole, tile), F32),
        vmem((batches, 2, whole, half), BF16),
        vmem((chunks, 2, 2, tok, half), BF16),
        vmem((chunks, tq, half), BF16),
        vmem((chunks, tok, half), F32),
        vmem((batches, 4, whole, fourth), F32),
        vmem((chunks, 2, th * fourth // 128 + 16, 128), BF16),
        vmem((chunks, 2, tok * fourth // 128 + 16, 128), BF16),
        vmem((chunks, 2, th * fourth // 128 + 16, 128), BF16),
        vmem((chunks, 2, tok * fourth // 128 + 16, 128), BF16),
        vmem((chunks, tok, tile), BF16),
        vmem((chunks, tok, half), F32),
        vmem((chunks, 2, tok, fourth), BF16),
        vmem((chunks, 2, 2, th, fourth), BF16),
        vmem((chunks, 2, tok, fourth), BF16),
        vmem((chunks, 2, 2, tok, half), F32),
        vmem((chunks, 2, tok, half), F32),
        vmem((chunks, 3, 2, tq, half), BF16),
        vmem((chunks, 2, 2, tq // 2, half), BF16),
        vmem((chunks, 2, 2, tq, half), BF16),
        vmem((chunks, 2, tq, half), F32),
        vmem((chunks, 2, tq * half // 128 + 16, 128), BF16),
        vmem((chunks, 3, tq * half // 128 + 16, 128), BF16),
        vmem((chunks, tq * half // 128 + 16, 128), BF16),
        vmem((chunks, tq * half // 128 + 16, 128), BF16),
        vmem((chunks, 2, tok, half), BF16),
        pltpu.SemaphoreType.DMA((N_REMOTE,)),
        pltpu.SemaphoreType.DMA((N_REMOTE,)),
        pltpu.SemaphoreType.DMA((N_LOCAL,)),
    ]
    anywhere = pl.BlockSpec(memory_space=pl.ANY)
    change = pl.pallas_call(
        kernel,
        out_shape=jax.ShapeDtypeStruct((1, batches, whole, tile), BF16),
        in_specs=[anywhere] * 4,
        out_specs=anywhere,
        scratch_shapes=scratch,
        compiler_params=pltpu.CompilerParams(
            collective_id=0, has_side_effects=True, vmem_limit_bytes=60_000_000
        ),
    )(grad_out, weight_in, weight_out, pre_act)
    return grad_out[None] + change.astype(F32)


def solution(mesh):
    return jax.shard_map(
        local,
        mesh=mesh,
        in_specs=(
            P(None, None, "wid"),
            P("section", "wid", "hid"),
            P("section", "hid", "wid"),
            P("section", None, None, "hid"),
        ),
        out_specs=P("section", None, None, "wid"),
        check_vma=False,
    )
```

```python
import functools

import jax
import jax.numpy as jnp
from jax import lax
from jax.experimental import pallas as pl
from jax.experimental.pallas import tpu as pltpu
from jax.sharding import PartitionSpec as P

F32 = jnp.float32
BF16 = jnp.bfloat16
MESH = pl.DeviceIdType.MESH
N_REMOTE = 272
N_LOCAL = 32
PIECES = 6
SPLIT = 2
START_DOWN = (0, 1, 2, 3)
START_UP = (0, 1, 2, 2)
NT = (((1,), (1,)), ((), ()))


def gelu_slope(pre):
    normal_cdf = 0.5 * (1.0 + lax.erf(pre * 0.7071067811865476))
    density = jnp.exp(-0.5 * pre * pre) * 0.3989422804014327
    return normal_cdf + pre * density


def pack(ref, value):
    rows, columns = value.shape
    blocks = [value[:, i : i + 128] for i in range(0, columns, 128)]
    top = functools.reduce(jnp.maximum, [jnp.max(jnp.abs(block), axis=0, keepdims=True) for block in blocks])
    scale = (80.0 / jnp.maximum(top, 1e-30)).astype(BF16)
    for i, block in enumerate(blocks):
        ref[rows * i : rows * (i + 1), :] = jnp.exp(block * scale.astype(F32)).astype(BF16)
    ref[rows * len(blocks) :, :] = jnp.broadcast_to(scale.astype(F32), (16, 128)).astype(BF16)


def unpack(ref, rows, columns):
    count = columns // 128
    step = 1.0 / ref[rows * count :, :].astype(F32)[:1]
    return jnp.concatenate(
        [jnp.log(ref[rows * i : rows * (i + 1), :].astype(F32)) * step for i in range(count)], axis=1
    )


def dot_nn(a, b):
    return lax.dot_general(a, b, (((1,), (0,)), ((), ())), preferred_element_type=F32)


def dot_nt(a, b):
    return lax.dot_general(a, b, NT, preferred_element_type=F32)


def kernel(
    grad, win, wout, pre, out,
    v_raw, w_raw, vt, wt, stripe, gbuf, gd, glow, gs, prev, pa, a1, a2, r1, r2, hid, pf, sb, rl, rp, pb, rc,
    xs1, xs2, xr1, xr2, xsum, zs, zr, ds, bs,
    send_sem, recv_sem, local_sem,
):
    s = lax.axis_index("section")
    h = lax.axis_index("hid")
    w = lax.axis_index("wid")
    x = lax.div(h, 4)
    zl = lax.rem(lax.div(h, 2), 2)
    core = lax.rem(h, 2)
    c = lax.div(w, 2)
    b = lax.rem(w, 2)
    tile = grad.shape[2]
    chunks, tok = pb.shape[0], pb.shape[3]
    half, fourth = tile // 2, tile // 4
    th, tq = tok // 2, tok // 4
    te = tq // 2

    def device(dx=0, dw=0, flip_core=False, flip_z=False, flip_s=False, flip_w=False):
        nx = lax.rem(x + dx + 4, 4) if dx else x
        nz = 1 - zl if flip_z else zl
        nc = 1 - core if flip_core else core
        nw = lax.rem(w + dw + 4, 4) if dw else w
        if flip_w:
            nw = w + 1 - 2 * b
        return {"section": 1 - s if flip_s else s, "hid": nx * 4 + nz * 2 + nc, "wid": nw}

    right, left = device(dx=1), device(dx=-1)
    up, down = device(dw=1), device(dw=-1)
    mate = device(flip_core=True)
    zmate = device(flip_z=True)
    wmate = device(flip_w=True)
    corner = device(flip_w=True, flip_z=True)
    cross = device(flip_s=True, flip_z=True)
    beyond = [cross, device(flip_s=True, flip_z=True, flip_w=True)]

    keys = {}

    def remote(key, src, dst, to):
        index = keys.setdefault(key, len(keys))
        return pltpu.make_async_remote_copy(
            src_ref=src, dst_ref=dst, send_sem=send_sem.at[index], recv_sem=recv_sem.at[index],
            device_id=to, device_id_type=MESH,
        )

    local_keys = {}

    def local(key, src, dst):
        index = local_keys.setdefault(key, len(local_keys))
        return pltpu.make_async_copy(src, dst, local_sem.at[index])

    def of4(i):
        return lax.rem(i + 4, 4)

    def cols(start, size):
        return pl.ds(pl.multiple_of(start, size), size)

    started = []

    def send(copy):
        copy.start()
        started.append(copy)
        return copy


    def span(m):
        return m // SPLIT, pl.ds(tok * (m % SPLIT), tok)

    pre_down = [
        local(("pre", m), pre.at[(0, *span(m), cols(fourth * w, fourth))], prev.at[m, :, pl.ds(0, fourth)])
        for m in range(chunks)
    ]
    pre_up = [
        local(("pre", m), pre.at[(0, *span(m), cols(half * b, half))], prev.at[m]) for m in range(chunks)
    ]
    v_loads = [
        local(("v", r), wout.at[0, cols(fourth * of4(w + r), fourth), :],
              v_raw.at[cols(fourth * of4(w + r), fourth), :])
        for r in (2, 1, 3, 0)
    ]
    w_load = local("w", win.at[0], w_raw)
    g_loads = [local(("g", m), grad.at[m], gbuf.at[m]) for m in range(chunks // SPLIT)]

    @pl.when(s == 0)
    def _():
        g_loads[0].start()

    for load in v_loads:
        load.start()
    w_load.start()

    @pl.when(s == 0)
    def _():
        for load in (*pre_down, *g_loads[1:]):
            load.start()

    @pl.when(s == 1)
    def _():
        for load in pre_up:
            load.start()

    barrier = pltpu.get_barrier_semaphore()
    peers = [right, left, up, down, mate, zmate, corner, *beyond]
    for peer in peers:
        pl.semaphore_signal(barrier, inc=1, device_id=peer, device_id_type=MESH)

    def all_in():
        pl.semaphore_wait(barrier, len(peers))

    def slope_stage(m, width):
        @pl.loop(0, 4)
        def _(i):
            rows = cols(i * (tok // 4), tok // 4)
            prev[m, rows, :width] = gelu_slope(prev[m, rows, :width])


    def core_send(m, q):
        return send(remote(("core", m, q), pb.at[m, q, 1 - core], rc.at[m, q], mate))

    def x_rows(r):
        return cols(tq * of4(x + r), tq)

    def chip_sum(m, q, r):
        rows = x_rows(r)
        return pb[m, q, core, rows, :] + rc[m, q, rows, :]

    def x_block(m, nq, r):
        return jnp.concatenate([chip_sum(m, q, r) for q in range(nq)], axis=1)

    def x_first(m, nq):
        total = x_block(m, nq, 2)
        used = pl.ds(0, te * nq * half // 128 + 16)
        copies = []
        for side, (name, to) in enumerate((("x1r", right), ("x1l", left))):
            pack(xs1.at[m, side, used], total[te * side : te * (side + 1)])
            copies.append(send(remote((name, m), xs1.at[m, side, used], xr1.at[m, side, used], to)))
        return copies

    def x_second(m, nq, first):
        result = []
        for side, (copy, r, to) in enumerate(((first[0], 1, right), (first[1], 3, left))):
            copy.wait_recv()
            total = x_block(m, nq, r)
            came = unpack(xr1.at[m, side, pl.ds(0, te * nq * half // 128 + 16)], te, nq * half)
            parts = [total[:te], total[te:]]
            parts[side] = parts[side] + came
            used = pl.ds(0, tq * nq * half // 128 + 16)
            pack(xs2.at[m, side, used], jnp.concatenate(parts, axis=0))
            result.append(send(remote(("x2", m, side), xs2.at[m, side, used], xr2.at[m, side, used], to)))
        return result

    def x_last(m, nq, second):
        total = x_block(m, nq, 0)
        for side, copy in enumerate(second):
            copy.wait_recv()
            total = total + unpack(xr2.at[m, side, pl.ds(0, tq * nq * half // 128 + 16)], tq, nq * half)
        for q in range(nq):
            xsum[m, q] = total[:, half * q : half * (q + 1)]


    def ring_gather(name, m, block):
        own = block(tq * x, tq)
        to_right = send(remote((name, "1r", m), own, own, right))
        to_left = send(remote((name, "1l", m), own, own, left))
        copies = [send(remote((name, "c0", m), own, own, mate))]
        yield
        to_right.wait_recv()
        piece = block(tq * of4(x - 1), te)
        on_right = send(remote((name, "2r", m), piece, piece, right))
        to_left.wait_recv()
        piece = block(tq * of4(x + 1) + te, te)
        on_left = send(remote((name, "2l", m), piece, piece, left))
        for i in (1, 3):
            piece = block(tq * of4(x + i), tq)
            copies.append(send(remote((name, "c", i, m), piece, piece, mate)))
        yield
        on_right.wait_recv()
        on_left.wait_recv()
        piece = block(tq * of4(x + 2), tq)
        copies.append(send(remote((name, "c2", m), piece, piece, mate)))
        yield copies

    def spread(m):
        for copies in ring_gather("o", m, lambda start, size: out.at[out_block(m, start, size)]):
            yield
        for copy in copies:
            copy.wait_recv()

    def out_block(m, start, size):
        first = tok * (m % SPLIT)
        return 0, m // SPLIT, pl.ds(pl.multiple_of(first + start, size), size), cols(half * core, half)

    def interleave(chain, start):
        steps = [chain(m) for m in range(chunks)]
        turn = 0
        alive = set(range(chunks))
        while alive:
            for m in sorted(alive):
                if turn >= start[m] and next(steps[m], alive) is alive:
                    alive.discard(m)
            turn += 1
        for copy in started:
            copy.wait_send()
        started.clear()


    def turn_weights(piece):
        if piece == 0:
            w_load.wait()

        @pl.loop(0, tile // 128 // PIECES)
        def _(i):
            columns = cols(128 * (tile // 128 // PIECES * piece + i), 128)
            for k in range(2):
                vt[k, columns, :] = w_raw[k * half : (k + 1) * half, columns].astype(F32).T.astype(BF16)

    def down_chain(m):
        batch, rows = m // SPLIT, pl.ds(tok * (m % SPLIT), tok)

        def partial(r):
            if m == 0:
                v_loads[(2, 1, 3, 0).index(r)].wait()
            units = cols(fourth * of4(w + r), fourth)
            pa[batch, r] = dot_nt(gd[batch, 0], v_raw[units, :half]) + dot_nt(gd[batch, 1], v_raw[units, half:])

        if m % SPLIT == 0:
            g_loads[batch].wait()
            for k in range(2):
                gd[batch, k] = gbuf[batch, :, k * half : (k + 1) * half].astype(BF16)
            partial(2)
        if m == 0:
            all_in()
        first = pa[batch, 2, rows]
        pack(a1.at[m, 0], first[:th])
        one = send(remote(("a1u", m), a1.at[m, 0], r1.at[m, 0], up))
        pack(a1.at[m, 1], first[th:])
        two = send(remote(("a1d", m), a1.at[m, 1], r1.at[m, 1], down))
        if m % SPLIT == 0:
            partial(1)
            partial(3)
        for piece in {0: (0, 1), 1: (2, 3), 2: (5,)}.get(m, ()):
            turn_weights(piece)
        yield
        one.wait_recv()
        part = pa[batch, 1, rows]
        pack(a2.at[m, 0], jnp.concatenate([part[:th] + unpack(r1.at[m, 0], th, fourth), part[th:]], axis=0))
        three = send(remote(("a2u", m), a2.at[m, 0], r2.at[m, 0], up))
        two.wait_recv()
        part = pa[batch, 3, rows]
        pack(a2.at[m, 1], jnp.concatenate([part[:th], part[th:] + unpack(r1.at[m, 1], th, fourth)], axis=0))
        four = send(remote(("a2d", m), a2.at[m, 1], r2.at[m, 1], down))
        if m % SPLIT == 0:
            partial(0)
        pre_down[m].wait()
        slope_stage(m, fourth)
        if m == 1:
            turn_weights(4)
        yield
        three.wait_recv()
        four.wait_recv()
        mine = cols(fourth * w, fourth)
        total = pa[batch, 0, rows] + unpack(r2.at[m, 0], tok, fourth) + unpack(r2.at[m, 1], tok, fourth)
        hid[m, :, mine] = (total * prev[m, :, :fourth]).astype(BF16)
        own = hid.at[m, :, mine]
        to_up = send(remote(("h1u", m), own, own, up))
        to_down = send(remote(("h1d", m), own, own, down))
        yield
        to_up.wait_recv()
        piece = hid.at[m, pl.ds(0, th), cols(fourth * of4(w - 1), fourth)]
        on_up = send(remote(("h2u", m), piece, piece, up))
        to_down.wait_recv()
        piece = hid.at[m, pl.ds(th, th), cols(fourth * of4(w + 1), fourth)]
        on_down = send(remote(("h2d", m), piece, piece, down))
        yield
        on_up.wait_recv()
        on_down.wait_recv()

        def product(k):
            pb[m, 0, k] = dot_nn(hid[m], vt[k])

        product(1 - core)
        copy = core_send(m, 0)
        product(core)
        yield
        copy.wait_recv()
        first = x_first(m, 1)
        yield
        second = x_second(m, 1, first)
        yield
        x_last(m, 1, second)
        pack(zs.at[m, 0], xsum[m, 0])
        copy = send(remote(("z", 0, m), zs.at[m, 0], zr.at[m, 0], zmate))
        yield
        copy.wait_recv()
        rows = cols(tq * x, tq)
        total = unpack(zs.at[m, 0], tq, half) + unpack(zr.at[m, 0], tq, half)
        grad_rows = pl.ds(pl.multiple_of(tok * (m % SPLIT) + tq * x, tq), tq)
        gs[m] = (total + gbuf[m // SPLIT, grad_rows, cols(half * core, half)]).astype(BF16)
        for copy in beyond_copies(m):
            send(copy)
        pack(ds.at[m], total)
        send(cross_copy(m))
        out[out_block(m, tq * x, tq)] = total.astype(BF16)
        yield from spread(m)

    def cross_copy(m):
        return remote(("cross", m), ds.at[m], bs.at[m], cross)

    def beyond_copies(m):
        return [
            remote(("beyond", i, m), gs.at[m], glow.at[m, b, core, cols(tq * x, tq)], to)
            for i, to in enumerate(beyond)
        ]

    @pl.when(s == 0)
    def _():
        interleave(down_chain, START_DOWN)


    def up_weights():
        for load in v_loads:
            load.wait()

        @pl.loop(0, tile // 128)
        def _(i):
            columns = cols(128 * i, 128)
            stripe[:tile, :] = v_raw[:, columns].astype(F32)
            for q in range(2):
                vt[q, columns, :] = stripe[pl.ds(q, half, stride=2), :].T.astype(BF16)

        w_load.wait()

        @pl.loop(0, half // 128)
        def _(i):
            for q in range(2):
                stripe[pl.ds(q, tile, stride=2), :] = w_raw[:, cols(half * q + 128 * i, 128)].astype(F32)
            wt[cols(128 * i, 128), :] = stripe[...].T.astype(BF16)

    def up_chain(m):
        for copy in beyond_copies(m):
            copy.wait_recv()
        for copies in ring_gather("g", m, lambda start, size: glow.at[m, :, core, cols(start, size)]):
            yield
        for copy in copies:
            copy.wait_recv()
        swaps = []
        for part in range(2):
            columns = pl.ds(fourth * part, fourth)
            total = None
            for q in range(2):
                for k in range(2):
                    term = dot_nn(glow[m, q, k], vt[q, k * half : (k + 1) * half, columns])
                    total = term if total is None else total + term
            pf[m, :, columns] = total
            pack(sb.at[m, part, 0], total[:th])
            one = send(remote(("p1u", m, part), sb.at[m, part, 0], rl.at[m, part, 0], up))
            pack(sb.at[m, part, 1], total[th:])
            two = send(remote(("p1d", m, part), sb.at[m, part, 1], rl.at[m, part, 1], down))
            swaps.append((one, two))
        yield
        relayed = []
        for part, (one, two) in enumerate(swaps):
            one.wait_recv()
            three = remote(("p2u", m, part), rl.at[m, part, 0], rp.at[m, part, 0], up)
            relayed.append(send(three))
            two.wait_recv()
            four = remote(("p2d", m, part), rl.at[m, part, 1], rp.at[m, part, 1], down)
            relayed.append(send(four))
        yield
        for copy in relayed:
            copy.wait_recv()
        for part in range(2):
            columns = pl.ds(fourth * part, fourth)
            came = [unpack(rp.at[m, part, i], th, fourth) for i in range(2)]
            total = pf[m, :, columns] + jnp.concatenate(came, axis=0)
            hid[m, :, columns] = (total * prev[m, :, columns]).astype(BF16)

        def product(q, k):
            pb[m, q, k] = dot_nn(hid[m, :, :half], wt[:, cols(tile * q + half * k, half)])

        copies = []
        for q in range(2):
            product(q, 1 - core)
            copies.append(core_send(m, q))
        for q in range(2):
            product(q, core)
        yield
        for copy in copies:
            copy.wait_recv()
        first = x_first(m, 2)
        yield
        second = x_second(m, 2, first)
        yield
        x_last(m, 2, second)
        pack(zs.at[m, 1], xsum[m, 1 - b])
        copies = [send(remote(("z", i, m), zs.at[m, 1], zr.at[m, i], to)) for i, to in ((2, corner), (1, wmate))]
        pack(zs.at[m, 0], xsum[m, b])
        copies.append(send(remote(("z", 0, m), zs.at[m, 0], zr.at[m, 0], zmate)))
        yield
        for copy in copies:
            copy.wait_recv()
        cross_copy(m).wait_recv()
        terms = [unpack(part, tq, half) for part in (zs.at[m, 0], zr.at[m, 0], zr.at[m, 1], zr.at[m, 2])]
        total = (terms[0] + terms[1]) + (terms[2] + terms[3])
        out[out_block(m, tq * x, tq)] = (total + unpack(bs.at[m], tq, half)).astype(BF16)
        yield from spread(m)

    @pl.when(s == 1)
    def _():
        up_weights()
        all_in()
        for m in range(chunks):
            pre_up[m].wait()
            slope_stage(m, half)
        interleave(up_chain, START_UP)


def local(grad_out, weight_in, weight_out, pre_act):
    batches, tok, tile = grad_out.shape
    chunks, whole, tok = batches * SPLIT, tok, tok // SPLIT
    half, fourth = tile // 2, tile // 4
    th, tq = tok // 2, tok // 4
    vmem = pltpu.VMEM
    scratch = [
        vmem((tile, tile), BF16),
        vmem((tile, tile), BF16),
        vmem((2, tile, half), BF16),
        vmem((half, 2 * tile), BF16),
        vmem((2 * tile, 128), F32),
        vmem((batches, whole, tile), F32),
        vmem((batches, 2, whole, half), BF16),
        vmem((chunks, 2, 2, tok, half), BF16),
        vmem((chunks, tq, half), BF16),
        vmem((chunks, tok, half), F32),
        vmem((batches, 4, whole, fourth), F32),
        vmem((chunks, 2, th * fourth // 128 + 16, 128), BF16),
        vmem((chunks, 2, tok * fourth // 128 + 16, 128), BF16),
        vmem((chunks, 2, th * fourth // 128 + 16, 128), BF16),
        vmem((chunks, 2, tok * fourth // 128 + 16, 128), BF16),
        vmem((chunks, tok, tile), BF16),
        vmem((chunks, tok, half), F32),
        vmem((chunks, 2, 2, th * fourth // 128 + 16, 128), BF16),
        vmem((chunks, 2, 2, th * fourth // 128 + 16, 128), BF16),
        vmem((chunks, 2, 2, th * fourth // 128 + 16, 128), BF16),
        vmem((chunks, 2, 2, tok, half), F32),
        vmem((chunks, 2, tok, half), F32),
        vmem((chunks, 2, tq * half // 128 + 16, 128), BF16),
        vmem((chunks, 2, tq * tile // 128 + 16, 128), BF16),
        vmem((chunks, 2, tq * half // 128 + 16, 128), BF16),
        vmem((chunks, 2, tq * tile // 128 + 16, 128), BF16),
        vmem((chunks, 2, tq, half), F32),
        vmem((chunks, 2, tq * half // 128 + 16, 128), BF16),
        vmem((chunks, 3, tq * half // 128 + 16, 128), BF16),
        vmem((chunks, tq * half // 128 + 16, 128), BF16),
        vmem((chunks, tq * half // 128 + 16, 128), BF16),
        pltpu.SemaphoreType.DMA((N_REMOTE,)),
        pltpu.SemaphoreType.DMA((N_REMOTE,)),
        pltpu.SemaphoreType.DMA((N_LOCAL,)),
    ]
    anywhere = pl.BlockSpec(memory_space=pl.ANY)
    change = pl.pallas_call(
        kernel,
        out_shape=vmem((1, batches, whole, tile), BF16),
        in_specs=[anywhere] * 4,
        out_specs=pl.BlockSpec(memory_space=vmem),
        scratch_shapes=scratch,
        compiler_params=pltpu.CompilerParams(
            collective_id=0, has_side_effects=True, vmem_limit_bytes=60_000_000
        ),
    )(grad_out, weight_in, weight_out, pre_act)
    return grad_out[None] + change.astype(F32)


def solution(mesh):
    return jax.shard_map(
        local,
        mesh=mesh,
        in_specs=(
            P(None, None, "wid"),
            P("section", "wid", "hid"),
            P("section", "hid", "wid"),
            P("section", None, None, "hid"),
        ),
        out_specs=P("section", None, None, "wid"),
        check_vma=False,
    )
```

```python
import functools

import jax
import jax.numpy as jnp
from jax import lax
from jax.experimental import pallas as pl
from jax.experimental.pallas import tpu as pltpu
from jax.sharding import PartitionSpec as P

F32 = jnp.float32
BF16 = jnp.bfloat16
MESH = pl.DeviceIdType.MESH
N_REMOTE = 272
N_LOCAL = 32
PIECES = 6
DIRECT = True
DIRECT_OUT = True
HOLD = 1
FAST = (0,)
SPLIT = 2
START_DOWN = (0, 1, 2, 3)
START_UP = (0, 1, 2, 2)
NT = (((1,), (1,)), ((), ()))


def gelu_slope(pre):
    normal_cdf = 0.5 * (1.0 + lax.erf(pre * 0.7071067811865476))
    density = jnp.exp(-0.5 * pre * pre) * 0.3989422804014327
    return normal_cdf + pre * density


def pack(ref, value):
    rows, columns = value.shape
    blocks = [value[:, i : i + 128] for i in range(0, columns, 128)]
    top = functools.reduce(jnp.maximum, [jnp.max(jnp.abs(block), axis=0, keepdims=True) for block in blocks])
    scale = (80.0 / jnp.maximum(top, 1e-30)).astype(BF16)
    for i, block in enumerate(blocks):
        ref[rows * i : rows * (i + 1), :] = jnp.exp(block * scale.astype(F32)).astype(BF16)
    ref[rows * len(blocks) :, :] = jnp.broadcast_to(scale.astype(F32), (16, 128)).astype(BF16)


def unpack(ref, rows, columns):
    count = columns // 128
    step = 1.0 / ref[rows * count :, :].astype(F32)[:1]
    return jnp.concatenate(
        [jnp.log(ref[rows * i : rows * (i + 1), :].astype(F32)) * step for i in range(count)], axis=1
    )


def dot_nn(a, b):
    return lax.dot_general(a, b, (((1,), (0,)), ((), ())), preferred_element_type=F32)


def dot_nt(a, b):
    return lax.dot_general(a, b, NT, preferred_element_type=F32)


def kernel(
    grad, win, wout, pre, out,
    v_raw, w_raw, vt, wt, stripe, gbuf, gd, glow, gs, prev, pa, a1, a2, r1, r2, hid, pf, sb, rl, rp, pb, rc,
    xs1, xs2, xr1, xr2, xr3, xsum, zs, zr, ds, bs,
    send_sem, recv_sem, local_sem,
):
    s = lax.axis_index("section")
    h = lax.axis_index("hid")
    w = lax.axis_index("wid")
    x = lax.div(h, 4)
    zl = lax.rem(lax.div(h, 2), 2)
    core = lax.rem(h, 2)
    c = lax.div(w, 2)
    b = lax.rem(w, 2)
    tile = grad.shape[2]
    chunks, tok = pb.shape[0], pb.shape[3]
    half, fourth = tile // 2, tile // 4
    th, tq = tok // 2, tok // 4
    te = tq // 2

    def device(dx=0, dw=0, flip_core=False, flip_z=False, flip_s=False, flip_w=False):
        nx = lax.rem(x + dx + 4, 4) if dx else x
        nz = 1 - zl if flip_z else zl
        nc = 1 - core if flip_core else core
        nw = lax.rem(w + dw + 4, 4) if dw else w
        if flip_w:
            nw = w + 1 - 2 * b
        return {"section": 1 - s if flip_s else s, "hid": nx * 4 + nz * 2 + nc, "wid": nw}

    right, left = device(dx=1), device(dx=-1)
    up, down = device(dw=1), device(dw=-1)
    mate = device(flip_core=True)
    zmate = device(flip_z=True)
    wmate = device(flip_w=True)
    corner = device(flip_w=True, flip_z=True)
    right_z, left_z = device(dx=1, flip_z=True), device(dx=-1, flip_z=True)
    right_mate, left_mate = device(dx=1, flip_core=True), device(dx=-1, flip_core=True)
    cross = device(flip_s=True, flip_z=True)
    beyond = [cross, device(flip_s=True, flip_z=True, flip_w=True)]

    keys = {}

    def remote(key, src, dst, to):
        index = keys.setdefault(key, len(keys))
        return pltpu.make_async_remote_copy(
            src_ref=src, dst_ref=dst, send_sem=send_sem.at[index], recv_sem=recv_sem.at[index],
            device_id=to, device_id_type=MESH,
        )

    local_keys = {}

    def local(key, src, dst):
        index = local_keys.setdefault(key, len(local_keys))
        return pltpu.make_async_copy(src, dst, local_sem.at[index])

    def of4(i):
        return lax.rem(i + 4, 4)

    def cols(start, size):
        return pl.ds(pl.multiple_of(start, size), size)

    started = []

    def send(copy):
        copy.start()
        started.append(copy)
        return copy


    def span(m):
        return m // SPLIT, pl.ds(tok * (m % SPLIT), tok)

    pre_down = [
        local(("pre", m), pre.at[(0, *span(m), cols(fourth * w, fourth))], prev.at[m, :, pl.ds(0, fourth)])
        for m in range(chunks)
    ]
    pre_up = [
        local(("pre", m), pre.at[(0, *span(m), cols(half * b, half))], prev.at[m]) for m in range(chunks)
    ]
    v_loads = [
        local(("v", r), wout.at[0, cols(fourth * of4(w + r), fourth), :],
              v_raw.at[cols(fourth * of4(w + r), fourth), :])
        for r in (2, 1, 3, 0)
    ]
    w_load = local("w", win.at[0], w_raw)
    g_loads = [local(("g", m), grad.at[m], gbuf.at[m]) for m in range(chunks // SPLIT)]

    @pl.when(s == 0)
    def _():
        g_loads[0].start()

    for load in v_loads:
        load.start()
    w_load.start()

    @pl.when(s == 0)
    def _():
        for load in (*pre_down, *g_loads[1:]):
            load.start()

    @pl.when(s == 1)
    def _():
        for load in pre_up:
            load.start()

    barrier = pltpu.get_barrier_semaphore()
    peers = [right, left, up, down, mate, zmate, corner, right_z, left_z, right_mate, left_mate, *beyond]
    for peer in peers:
        pl.semaphore_signal(barrier, inc=1, device_id=peer, device_id_type=MESH)

    def all_in():
        pl.semaphore_wait(barrier, len(peers))

    def slope_stage(m, width):
        @pl.loop(0, 4)
        def _(i):
            rows = cols(i * (tok // 4), tok // 4)
            prev[m, rows, :width] = gelu_slope(prev[m, rows, :width])


    def core_send(m, q):
        return send(remote(("core", m, q), pb.at[m, q, 1 - core], rc.at[m, q], mate))

    def x_rows(r):
        return cols(tq * of4(x + r), tq)

    def chip_sum(m, q, r):
        rows = x_rows(r)
        return pb[m, q, core, rows, :] + rc[m, q, rows, :]

    def x_block(m, nq, r):
        return jnp.concatenate([chip_sum(m, q, r) for q in range(nq)], axis=1)

    def x_first(m, nq):
        total = x_block(m, nq, 2)
        used = pl.ds(0, te * nq * half // 128 + 16)
        copies = []
        for side, (name, to) in enumerate((("x1r", right), ("x1l", left))):
            pack(xs1.at[m, side, used], total[te * side : te * (side + 1)])
            copies.append(send(remote((name, m), xs1.at[m, side, used], xr1.at[m, side, used], to)))
        return copies

    def x_second(m, nq, first, twins=()):
        result = []
        for side, (copy, r, to) in enumerate(((first[0], 1, right), (first[1], 3, left))):
            copy.wait_recv()
            total = x_block(m, nq, r)
            came = unpack(xr1.at[m, side, pl.ds(0, te * nq * half // 128 + 16)], te, nq * half)
            parts = [total[:te], total[te:]]
            parts[side] = parts[side] + came
            used = pl.ds(0, tq * nq * half // 128 + 16)
            pack(xs2.at[m, side, used], jnp.concatenate(parts, axis=0))
            result.append(send(remote(("x2", m, side), xs2.at[m, side, used], xr2.at[m, side, used], to)))
        for side, to in enumerate(twins):
            used = pl.ds(0, tq * nq * half // 128 + 16)
            result.append(send(remote(("x3", m, side), xs2.at[m, side, used], xr3.at[m, side], to)))
        return result

    def x_last(m, nq, second):
        total = x_block(m, nq, 0)
        for side, copy in enumerate(second):
            copy.wait_recv()
            total = total + unpack(xr2.at[m, side, pl.ds(0, tq * nq * half // 128 + 16)], tq, nq * half)
        for q in range(nq):
            xsum[m, q] = total[:, half * q : half * (q + 1)]


    def ring_gather(name, m, block, direct):
        own = block(tq * x, tq)
        to_right = send(remote((name, "1r", m), own, own, right))
        to_left = send(remote((name, "1l", m), own, own, left))
        copies = [send(remote((name, "c0", m), own, own, mate))]
        yield
        to_right.wait_recv()
        piece = block(tq * of4(x - 1), te)
        on_right = send(remote((name, "2r", m), piece, piece, right))
        to_left.wait_recv()
        piece = block(tq * of4(x + 1) + te, te)
        on_left = send(remote((name, "2l", m), piece, piece, left))
        for i in (1, 3):
            piece = block(tq * of4(x + i), tq)
            copies.append(send(remote((name, "c", i, m), piece, piece, mate)))
        if direct:
            piece = block(tq * of4(x - 1), te)
            copies.append(send(remote((name, "3r", m), piece, piece, right_mate)))
            piece = block(tq * of4(x + 1) + te, te)
            copies.append(send(remote((name, "3l", m), piece, piece, left_mate)))
        yield
        on_right.wait_recv()
        on_left.wait_recv()
        if not direct:
            piece = block(tq * of4(x + 2), tq)
            copies.append(send(remote((name, "c2", m), piece, piece, mate)))
            yield
        return copies

    def spread(m):
        copies = yield from ring_gather("o", m, lambda start, size: out.at[out_block(m, start, size)], DIRECT_OUT)
        for copy in copies:
            copy.wait_recv()

    def out_block(m, start, size):
        first = tok * (m % SPLIT)
        return 0, m // SPLIT, pl.ds(pl.multiple_of(first + start, size), size), cols(half * core, half)

    def interleave(chain, start):
        steps = [chain(m) for m in range(chunks)]
        turn = 0
        alive = set(range(chunks))
        while alive:
            for m in sorted(alive):
                if turn >= start[m] and next(steps[m], alive) is alive:
                    alive.discard(m)
            turn += 1
        for copy in started:
            copy.wait_send()
        started.clear()


    def turn_weights(piece):
        if piece == 0:
            w_load.wait()

        @pl.loop(0, tile // 128 // PIECES)
        def _(i):
            columns = cols(128 * (tile // 128 // PIECES * piece + i), 128)
            for k in range(2):
                vt[k, columns, :] = w_raw[k * half : (k + 1) * half, columns].astype(F32).T.astype(BF16)

    def down_chain(m):
        batch, rows = m // SPLIT, pl.ds(tok * (m % SPLIT), tok)

        def partial(r):
            if m == 0:
                v_loads[(2, 1, 3, 0).index(r)].wait()
            units = cols(fourth * of4(w + r), fourth)
            pa[batch, r] = dot_nt(gd[batch, 0], v_raw[units, :half]) + dot_nt(gd[batch, 1], v_raw[units, half:])

        if m % SPLIT == 0:
            g_loads[batch].wait()
            for k in range(2):
                gd[batch, k] = gbuf[batch, :, k * half : (k + 1) * half].astype(BF16)
            partial(2)
        if m == 0:
            all_in()
        first = pa[batch, 2, rows]
        pack(a1.at[m, 0], first[:th])
        one = send(remote(("a1u", m), a1.at[m, 0], r1.at[m, 0], up))
        pack(a1.at[m, 1], first[th:])
        two = send(remote(("a1d", m), a1.at[m, 1], r1.at[m, 1], down))
        if m % SPLIT == 0:
            partial(1)
            partial(3)
        for piece in {0: (0, 1), 1: (2, 3), 2: (5,)}.get(m, ()):
            turn_weights(piece)
        yield
        one.wait_recv()
        part = pa[batch, 1, rows]
        pack(a2.at[m, 0], jnp.concatenate([part[:th] + unpack(r1.at[m, 0], th, fourth), part[th:]], axis=0))
        three = send(remote(("a2u", m), a2.at[m, 0], r2.at[m, 0], up))
        two.wait_recv()
        part = pa[batch, 3, rows]
        pack(a2.at[m, 1], jnp.concatenate([part[:th], part[th:] + unpack(r1.at[m, 1], th, fourth)], axis=0))
        four = send(remote(("a2d", m), a2.at[m, 1], r2.at[m, 1], down))
        if m % SPLIT == 0:
            partial(0)
        pre_down[m].wait()
        slope_stage(m, fourth)
        if m == 1:
            turn_weights(4)
        yield
        three.wait_recv()
        four.wait_recv()
        mine = cols(fourth * w, fourth)
        total = pa[batch, 0, rows] + unpack(r2.at[m, 0], tok, fourth) + unpack(r2.at[m, 1], tok, fourth)
        hid[m, :, mine] = (total * prev[m, :, :fourth]).astype(BF16)
        own = hid.at[m, :, mine]
        to_up = send(remote(("h1u", m), own, own, up))
        to_down = send(remote(("h1d", m), own, own, down))
        yield
        to_up.wait_recv()
        piece = hid.at[m, pl.ds(0, th), cols(fourth * of4(w - 1), fourth)]
        on_up = send(remote(("h2u", m), piece, piece, up))
        to_down.wait_recv()
        piece = hid.at[m, pl.ds(th, th), cols(fourth * of4(w + 1), fourth)]
        on_down = send(remote(("h2d", m), piece, piece, down))
        yield
        on_up.wait_recv()
        on_down.wait_recv()

        def product(k):
            pb[m, 0, k] = dot_nn(hid[m], vt[k])

        product(1 - core)
        copy = core_send(m, 0)
        product(core)
        yield
        copy.wait_recv()
        first = x_first(m, 1)
        yield
        rows = cols(tq * x, tq)
        if m in FAST:
            copies = x_second(m, 1, first, (right_z, left_z))
            pack(zs.at[m, 0], x_block(m, 1, 0))
            copies.append(send(remote(("z", 0, m), zs.at[m, 0], zr.at[m, 0], zmate)))
            yield
            for copy in copies:
                copy.wait_recv()
            used = pl.ds(0, tq * half // 128 + 16)
            here = [unpack(part, tq, half) for part in (zs.at[m, 0], xr2.at[m, 0, used], xr2.at[m, 1, used])]
            there = [unpack(part, tq, half) for part in (zr.at[m, 0], xr3.at[m, 0], xr3.at[m, 1])]
            total = (here[0] + here[1] + here[2]) + (there[0] + there[1] + there[2])
        else:
            second = x_second(m, 1, first)
            yield
            x_last(m, 1, second)
            pack(zs.at[m, 0], xsum[m, 0])
            copy = send(remote(("z", 0, m), zs.at[m, 0], zr.at[m, 0], zmate))
            yield
            copy.wait_recv()
            total = unpack(zs.at[m, 0], tq, half) + unpack(zr.at[m, 0], tq, half)
        grad_rows = pl.ds(pl.multiple_of(tok * (m % SPLIT) + tq * x, tq), tq)
        gs[m] = (total + gbuf[m // SPLIT, grad_rows, cols(half * core, half)]).astype(BF16)
        for copy in beyond_copies(m):
            send(copy)
        pack(ds.at[m], total)
        send(cross_copy(m))
        out[out_block(m, tq * x, tq)] = total.astype(BF16)
        for _ in range(HOLD * (chunks - 1 - m)):
            yield
        yield from spread(m)

    def cross_copy(m):
        return remote(("cross", m), ds.at[m], bs.at[m], cross)

    def beyond_copies(m):
        return [
            remote(("beyond", i, m), gs.at[m], glow.at[m, b, core, cols(tq * x, tq)], to)
            for i, to in enumerate(beyond)
        ]

    @pl.when(s == 0)
    def _():
        interleave(down_chain, START_DOWN)


    def up_weights():
        for load in v_loads:
            load.wait()

        @pl.loop(0, tile // 128)
        def _(i):
            columns = cols(128 * i, 128)
            stripe[:tile, :] = v_raw[:, columns].astype(F32)
            for q in range(2):
                vt[q, columns, :] = stripe[pl.ds(q, half, stride=2), :].T.astype(BF16)

        w_load.wait()

        @pl.loop(0, half // 128)
        def _(i):
            for q in range(2):
                stripe[pl.ds(q, tile, stride=2), :] = w_raw[:, cols(half * q + 128 * i, 128)].astype(F32)
            wt[cols(128 * i, 128), :] = stripe[...].T.astype(BF16)

    def up_chain(m):
        for copy in beyond_copies(m):
            copy.wait_recv()
        copies = yield from ring_gather("g", m, lambda start, size: glow.at[m, :, core, cols(start, size)], DIRECT)
        for copy in copies:
            copy.wait_recv()
        swaps = []
        for part in range(2):
            columns = pl.ds(fourth * part, fourth)
            total = None
            for q in range(2):
                for k in range(2):
                    term = dot_nn(glow[m, q, k], vt[q, k * half : (k + 1) * half, columns])
                    total = term if total is None else total + term
            pf[m, :, columns] = total
            pack(sb.at[m, part, 0], total[:th])
            one = send(remote(("p1u", m, part), sb.at[m, part, 0], rl.at[m, part, 0], up))
            pack(sb.at[m, part, 1], total[th:])
            two = send(remote(("p1d", m, part), sb.at[m, part, 1], rl.at[m, part, 1], down))
            swaps.append((one, two))
        yield
        relayed = []
        for part, (one, two) in enumerate(swaps):
            one.wait_recv()
            three = remote(("p2u", m, part), rl.at[m, part, 0], rp.at[m, part, 0], up)
            relayed.append(send(three))
            two.wait_recv()
            four = remote(("p2d", m, part), rl.at[m, part, 1], rp.at[m, part, 1], down)
            relayed.append(send(four))
        yield
        for copy in relayed:
            copy.wait_recv()
        for part in range(2):
            columns = pl.ds(fourth * part, fourth)
            came = [unpack(rp.at[m, part, i], th, fourth) for i in range(2)]
            total = pf[m, :, columns] + jnp.concatenate(came, axis=0)
            hid[m, :, columns] = (total * prev[m, :, columns]).astype(BF16)

        def product(q, k):
            pb[m, q, k] = dot_nn(hid[m, :, :half], wt[:, cols(tile * q + half * k, half)])

        copies = []
        for q in range(2):
            product(q, 1 - core)
            copies.append(core_send(m, q))
        for q in range(2):
            product(q, core)
        yield
        for copy in copies:
            copy.wait_recv()
        first = x_first(m, 2)
        yield
        second = x_second(m, 2, first)
        yield
        x_last(m, 2, second)
        pack(zs.at[m, 1], xsum[m, 1 - b])
        copies = [send(remote(("z", i, m), zs.at[m, 1], zr.at[m, i], to)) for i, to in ((2, corner), (1, wmate))]
        pack(zs.at[m, 0], xsum[m, b])
        copies.append(send(remote(("z", 0, m), zs.at[m, 0], zr.at[m, 0], zmate)))
        yield
        for copy in copies:
            copy.wait_recv()
        cross_copy(m).wait_recv()
        terms = [unpack(part, tq, half) for part in (zs.at[m, 0], zr.at[m, 0], zr.at[m, 1], zr.at[m, 2])]
        total = (terms[0] + terms[1]) + (terms[2] + terms[3])
        out[out_block(m, tq * x, tq)] = (total + unpack(bs.at[m], tq, half)).astype(BF16)
        yield from spread(m)

    @pl.when(s == 1)
    def _():
        up_weights()
        all_in()
        for m in range(chunks):
            pre_up[m].wait()
            slope_stage(m, half)
        interleave(up_chain, START_UP)


def local(grad_out, weight_in, weight_out, pre_act):
    batches, tok, tile = grad_out.shape
    chunks, whole, tok = batches * SPLIT, tok, tok // SPLIT
    half, fourth = tile // 2, tile // 4
    th, tq = tok // 2, tok // 4
    vmem = pltpu.VMEM
    scratch = [
        vmem((tile, tile), BF16),
        vmem((tile, tile), BF16),
        vmem((2, tile, half), BF16),
        vmem((half, 2 * tile), BF16),
        vmem((2 * tile, 128), F32),
        vmem((batches, whole, tile), F32),
        vmem((batches, 2, whole, half), BF16),
        vmem((chunks, 2, 2, tok, half), BF16),
        vmem((chunks, tq, half), BF16),
        vmem((chunks, tok, half), F32),
        vmem((batches, 4, whole, fourth), F32),
        vmem((chunks, 2, th * fourth // 128 + 16, 128), BF16),
        vmem((chunks, 2, tok * fourth // 128 + 16, 128), BF16),
        vmem((chunks, 2, th * fourth // 128 + 16, 128), BF16),
        vmem((chunks, 2, tok * fourth // 128 + 16, 128), BF16),
        vmem((chunks, tok, tile), BF16),
        vmem((chunks, tok, half), F32),
        vmem((chunks, 2, 2, th * fourth // 128 + 16, 128), BF16),
        vmem((chunks, 2, 2, th * fourth // 128 + 16, 128), BF16),
        vmem((chunks, 2, 2, th * fourth // 128 + 16, 128), BF16),
        vmem((chunks, 2, 2, tok, half), F32),
        vmem((chunks, 2, tok, half), F32),
        vmem((chunks, 2, tq * half // 128 + 16, 128), BF16),
        vmem((chunks, 2, tq * tile // 128 + 16, 128), BF16),
        vmem((chunks, 2, tq * half // 128 + 16, 128), BF16),
        vmem((chunks, 2, tq * tile // 128 + 16, 128), BF16),
        vmem((chunks, 2, tq * half // 128 + 16, 128), BF16),
        vmem((chunks, 2, tq, half), F32),
        vmem((chunks, 2, tq * half // 128 + 16, 128), BF16),
        vmem((chunks, 3, tq * half // 128 + 16, 128), BF16),
        vmem((chunks, tq * half // 128 + 16, 128), BF16),
        vmem((chunks, tq * half // 128 + 16, 128), BF16),
        pltpu.SemaphoreType.DMA((N_REMOTE,)),
        pltpu.SemaphoreType.DMA((N_REMOTE,)),
        pltpu.SemaphoreType.DMA((N_LOCAL,)),
    ]
    anywhere = pl.BlockSpec(memory_space=pl.ANY)
    change = pl.pallas_call(
        kernel,
        out_shape=vmem((1, batches, whole, tile), BF16),
        in_specs=[anywhere] * 4,
        out_specs=pl.BlockSpec(memory_space=vmem),
        scratch_shapes=scratch,
        compiler_params=pltpu.CompilerParams(
            collective_id=0, has_side_effects=True, vmem_limit_bytes=60_000_000
        ),
    )(grad_out, weight_in, weight_out, pre_act)
    return grad_out[None] + change.astype(F32)


def solution(mesh):
    return jax.shard_map(
        local,
        mesh=mesh,
        in_specs=(
            P(None, None, "wid"),
            P("section", "wid", "hid"),
            P("section", "hid", "wid"),
            P("section", None, None, "hid"),
        ),
        out_specs=P("section", None, None, "wid"),
        check_vma=False,
    )
```

```python
import functools

import jax
import jax.numpy as jnp
from jax import lax
from jax.experimental import pallas as pl
from jax.experimental.pallas import tpu as pltpu
from jax.sharding import PartitionSpec as P

F32 = jnp.float32
BF16 = jnp.bfloat16
MESH = pl.DeviceIdType.MESH
N_REMOTE = 272
N_LOCAL = 32
PIECES = 6
DIRECT = True
DIRECT_OUT = False
HOLD = 1
FAST = (0,)
SPLIT = 2
START_DOWN = (0, 1, 2, 3)
START_UP = (0, 1, 2, 3)
NT = (((1,), (1,)), ((), ()))


def gelu_slope(pre):
    normal_cdf = 0.5 * (1.0 + lax.erf(pre * 0.7071067811865476))
    density = jnp.exp(-0.5 * pre * pre) * 0.3989422804014327
    return normal_cdf + pre * density


def pack(ref, value):
    rows, columns = value.shape
    blocks = [value[:, i : i + 128] for i in range(0, columns, 128)]
    top = functools.reduce(jnp.maximum, [jnp.max(jnp.abs(block), axis=0, keepdims=True) for block in blocks])
    scale = (80.0 / jnp.maximum(top, 1e-30)).astype(BF16)
    for i, block in enumerate(blocks):
        ref[rows * i : rows * (i + 1), :] = jnp.exp(block * scale.astype(F32)).astype(BF16)
    ref[rows * len(blocks) :, :] = jnp.broadcast_to(scale.astype(F32), (16, 128)).astype(BF16)


def unpack(ref, rows, columns):
    count = columns // 128
    step = 1.0 / ref[rows * count :, :].astype(F32)[:1]
    return jnp.concatenate(
        [jnp.log(ref[rows * i : rows * (i + 1), :].astype(F32)) * step for i in range(count)], axis=1
    )


def dot_nn(a, b):
    return lax.dot_general(a, b, (((1,), (0,)), ((), ())), preferred_element_type=F32)


def dot_nt(a, b):
    return lax.dot_general(a, b, NT, preferred_element_type=F32)


def kernel(
    grad, win, wout, pre, out,
    v_raw, w_raw, vt, wt, stripe, gbuf, gd, glow, gs, prev, pa, a1, a2, r1, r2, hid, pf, sb, rl, rp, pb, rc,
    xs1, xs2, xr1, xr2, xr3, xsum, zs, zr, ds, bs,
    send_sem, recv_sem, local_sem,
):
    s = lax.axis_index("section")
    h = lax.axis_index("hid")
    w = lax.axis_index("wid")
    x = lax.div(h, 4)
    zl = lax.rem(lax.div(h, 2), 2)
    core = lax.rem(h, 2)
    c = lax.div(w, 2)
    b = lax.rem(w, 2)
    tile = grad.shape[2]
    chunks, tok = pb.shape[0], pb.shape[3]
    half, fourth = tile // 2, tile // 4
    th, tq = tok // 2, tok // 4
    te = tq // 2

    def device(dx=0, dw=0, flip_core=False, flip_z=False, flip_s=False, flip_w=False):
        nx = lax.rem(x + dx + 4, 4) if dx else x
        nz = 1 - zl if flip_z else zl
        nc = 1 - core if flip_core else core
        nw = lax.rem(w + dw + 4, 4) if dw else w
        if flip_w:
            nw = w + 1 - 2 * b
        return {"section": 1 - s if flip_s else s, "hid": nx * 4 + nz * 2 + nc, "wid": nw}

    right, left = device(dx=1), device(dx=-1)
    up, down = device(dw=1), device(dw=-1)
    mate = device(flip_core=True)
    zmate = device(flip_z=True)
    wmate = device(flip_w=True)
    corner = device(flip_w=True, flip_z=True)
    right_z, left_z = device(dx=1, flip_z=True), device(dx=-1, flip_z=True)
    right_mate, left_mate = device(dx=1, flip_core=True), device(dx=-1, flip_core=True)
    cross = device(flip_s=True, flip_z=True)
    beyond = [cross, device(flip_s=True, flip_z=True, flip_w=True)]

    keys = {}

    def remote(key, src, dst, to):
        index = keys.setdefault(key, len(keys))
        return pltpu.make_async_remote_copy(
            src_ref=src, dst_ref=dst, send_sem=send_sem.at[index], recv_sem=recv_sem.at[index],
            device_id=to, device_id_type=MESH,
        )

    local_keys = {}

    def local(key, src, dst):
        index = local_keys.setdefault(key, len(local_keys))
        return pltpu.make_async_copy(src, dst, local_sem.at[index])

    def of4(i):
        return lax.rem(i + 4, 4)

    def cols(start, size):
        return pl.ds(pl.multiple_of(start, size), size)

    started = []

    def send(copy):
        copy.start()
        started.append(copy)
        return copy


    def span(m):
        return m // SPLIT, pl.ds(tok * (m % SPLIT), tok)

    pre_down = [
        local(("pre", m), pre.at[(0, *span(m), cols(fourth * w, fourth))], prev.at[m, :, pl.ds(0, fourth)])
        for m in range(chunks)
    ]
    pre_up = [
        local(("pre", m), pre.at[(0, *span(m), cols(half * b, half))], prev.at[m]) for m in range(chunks)
    ]
    v_loads = [
        local(("v", r), wout.at[0, cols(fourth * of4(w + r), fourth), :],
              v_raw.at[cols(fourth * of4(w + r), fourth), :])
        for r in (2, 1, 3, 0)
    ]
    w_load = local("w", win.at[0], w_raw)
    g_loads = [local(("g", m), grad.at[m], gbuf.at[m]) for m in range(chunks // SPLIT)]

    @pl.when(s == 0)
    def _():
        g_loads[0].start()

    for load in v_loads:
        load.start()
    w_load.start()

    @pl.when(s == 0)
    def _():
        for load in (*pre_down, *g_loads[1:]):
            load.start()

    @pl.when(s == 1)
    def _():
        for load in pre_up:
            load.start()

    barrier = pltpu.get_barrier_semaphore()
    peers = [right, left, up, down, mate, zmate, corner, right_z, left_z, right_mate, left_mate, *beyond]
    for peer in peers:
        pl.semaphore_signal(barrier, inc=1, device_id=peer, device_id_type=MESH)

    def all_in():
        pl.semaphore_wait(barrier, len(peers))

    def slope_stage(m, width):
        @pl.loop(0, 4)
        def _(i):
            rows = cols(i * (tok // 4), tok // 4)
            prev[m, rows, :width] = gelu_slope(prev[m, rows, :width])


    def core_send(m, q):
        return send(remote(("core", m, q), pb.at[m, q, 1 - core], rc.at[m, q], mate))

    def x_rows(r):
        return cols(tq * of4(x + r), tq)

    def chip_sum(m, q, r):
        rows = x_rows(r)
        return pb[m, q, core, rows, :] + rc[m, q, rows, :]

    def x_block(m, nq, r):
        return jnp.concatenate([chip_sum(m, q, r) for q in range(nq)], axis=1)

    def x_first(m, nq):
        total = x_block(m, nq, 2)
        used = pl.ds(0, te * nq * half // 128 + 16)
        copies = []
        for side, (name, to) in enumerate((("x1r", right), ("x1l", left))):
            pack(xs1.at[m, side, used], total[te * side : te * (side + 1)])
            copies.append(send(remote((name, m), xs1.at[m, side, used], xr1.at[m, side, used], to)))
        return copies

    def x_second(m, nq, first, twins=()):
        result = []
        for side, (copy, r, to) in enumerate(((first[0], 1, right), (first[1], 3, left))):
            copy.wait_recv()
            total = x_block(m, nq, r)
            came = unpack(xr1.at[m, side, pl.ds(0, te * nq * half // 128 + 16)], te, nq * half)
            parts = [total[:te], total[te:]]
            parts[side] = parts[side] + came
            used = pl.ds(0, tq * nq * half // 128 + 16)
            pack(xs2.at[m, side, used], jnp.concatenate(parts, axis=0))
            result.append(send(remote(("x2", m, side), xs2.at[m, side, used], xr2.at[m, side, used], to)))
        for side, to in enumerate(twins):
            used = pl.ds(0, tq * nq * half // 128 + 16)
            result.append(send(remote(("x3", m, side), xs2.at[m, side, used], xr3.at[m, side], to)))
        return result

    def x_last(m, nq, second):
        total = x_block(m, nq, 0)
        for side, copy in enumerate(second):
            copy.wait_recv()
            total = total + unpack(xr2.at[m, side, pl.ds(0, tq * nq * half // 128 + 16)], tq, nq * half)
        for q in range(nq):
            xsum[m, q] = total[:, half * q : half * (q + 1)]


    def ring_gather(name, m, block, direct):
        own = block(tq * x, tq)
        to_right = send(remote((name, "1r", m), own, own, right))
        to_left = send(remote((name, "1l", m), own, own, left))
        copies = [send(remote((name, "c0", m), own, own, mate))]
        yield
        to_right.wait_recv()
        piece = block(tq * of4(x - 1), te)
        on_right = send(remote((name, "2r", m), piece, piece, right))
        to_left.wait_recv()
        piece = block(tq * of4(x + 1) + te, te)
        on_left = send(remote((name, "2l", m), piece, piece, left))
        for i in (1, 3):
            piece = block(tq * of4(x + i), tq)
            copies.append(send(remote((name, "c", i, m), piece, piece, mate)))
        if direct:
            piece = block(tq * of4(x - 1), te)
            copies.append(send(remote((name, "3r", m), piece, piece, right_mate)))
            piece = block(tq * of4(x + 1) + te, te)
            copies.append(send(remote((name, "3l", m), piece, piece, left_mate)))
        yield
        on_right.wait_recv()
        on_left.wait_recv()
        if not direct:
            piece = block(tq * of4(x + 2), tq)
            copies.append(send(remote((name, "c2", m), piece, piece, mate)))
            yield
        return copies

    def spread(m):
        copies = yield from ring_gather("o", m, lambda start, size: out.at[out_block(m, start, size)], DIRECT_OUT)
        for copy in copies:
            copy.wait_recv()

    def out_block(m, start, size):
        first = tok * (m % SPLIT)
        return 0, m // SPLIT, pl.ds(pl.multiple_of(first + start, size), size), cols(half * core, half)

    def interleave(chain, start):
        steps = [chain(m) for m in range(chunks)]
        turn = 0
        alive = set(range(chunks))
        while alive:
            for m in sorted(alive):
                if turn >= start[m] and next(steps[m], alive) is alive:
                    alive.discard(m)
            turn += 1
        for copy in started:
            copy.wait_send()
        started.clear()


    def turn_weights(piece):
        if piece == 0:
            w_load.wait()

        @pl.loop(0, tile // 128 // PIECES)
        def _(i):
            columns = cols(128 * (tile // 128 // PIECES * piece + i), 128)
            for k in range(2):
                vt[k, columns, :] = w_raw[k * half : (k + 1) * half, columns].astype(F32).T.astype(BF16)

    def down_chain(m):
        batch, rows = m // SPLIT, pl.ds(tok * (m % SPLIT), tok)

        def partial(r):
            if m == 0:
                v_loads[(2, 1, 3, 0).index(r)].wait()
            units = cols(fourth * of4(w + r), fourth)
            pa[batch, r] = dot_nt(gd[batch, 0], v_raw[units, :half]) + dot_nt(gd[batch, 1], v_raw[units, half:])

        if m % SPLIT == 0:
            g_loads[batch].wait()
            for k in range(2):
                gd[batch, k] = gbuf[batch, :, k * half : (k + 1) * half].astype(BF16)
            partial(2)
        if m == 0:
            all_in()
        first = pa[batch, 2, rows]
        pack(a1.at[m, 0], first[:th])
        one = send(remote(("a1u", m), a1.at[m, 0], r1.at[m, 0], up))
        pack(a1.at[m, 1], first[th:])
        two = send(remote(("a1d", m), a1.at[m, 1], r1.at[m, 1], down))
        if m % SPLIT == 0:
            partial(1)
            partial(3)
        for piece in {0: (0, 1), 1: (2, 3), 2: (5,)}.get(m, ()):
            turn_weights(piece)
        yield
        one.wait_recv()
        part = pa[batch, 1, rows]
        pack(a2.at[m, 0], jnp.concatenate([part[:th] + unpack(r1.at[m, 0], th, fourth), part[th:]], axis=0))
        three = send(remote(("a2u", m), a2.at[m, 0], r2.at[m, 0], up))
        two.wait_recv()
        part = pa[batch, 3, rows]
        pack(a2.at[m, 1], jnp.concatenate([part[:th], part[th:] + unpack(r1.at[m, 1], th, fourth)], axis=0))
        four = send(remote(("a2d", m), a2.at[m, 1], r2.at[m, 1], down))
        if m % SPLIT == 0:
            partial(0)
        pre_down[m].wait()
        slope_stage(m, fourth)
        if m == 1:
            turn_weights(4)
        yield
        three.wait_recv()
        four.wait_recv()
        mine = cols(fourth * w, fourth)
        total = pa[batch, 0, rows] + unpack(r2.at[m, 0], tok, fourth) + unpack(r2.at[m, 1], tok, fourth)
        hid[m, :, mine] = (total * prev[m, :, :fourth]).astype(BF16)
        own = hid.at[m, :, mine]
        to_up = send(remote(("h1u", m), own, own, up))
        to_down = send(remote(("h1d", m), own, own, down))
        yield
        to_up.wait_recv()
        piece = hid.at[m, pl.ds(0, th), cols(fourth * of4(w - 1), fourth)]
        on_up = send(remote(("h2u", m), piece, piece, up))
        to_down.wait_recv()
        piece = hid.at[m, pl.ds(th, th), cols(fourth * of4(w + 1), fourth)]
        on_down = send(remote(("h2d", m), piece, piece, down))
        yield
        on_up.wait_recv()
        on_down.wait_recv()

        def product(k):
            pb[m, 0, k] = dot_nn(hid[m], vt[k])

        product(1 - core)
        copy = core_send(m, 0)
        product(core)
        yield
        copy.wait_recv()
        first = x_first(m, 1)
        yield
        rows = cols(tq * x, tq)
        if m in FAST:
            copies = x_second(m, 1, first, (right_z, left_z))
            pack(zs.at[m, 0], x_block(m, 1, 0))
            copies.append(send(remote(("z", 0, m), zs.at[m, 0], zr.at[m, 0], zmate)))
            yield
            for copy in copies:
                copy.wait_recv()
            used = pl.ds(0, tq * half // 128 + 16)
            here = [unpack(part, tq, half) for part in (zs.at[m, 0], xr2.at[m, 0, used], xr2.at[m, 1, used])]
            there = [unpack(part, tq, half) for part in (zr.at[m, 0], xr3.at[m, 0], xr3.at[m, 1])]
            total = (here[0] + here[1] + here[2]) + (there[0] + there[1] + there[2])
        else:
            second = x_second(m, 1, first)
            yield
            x_last(m, 1, second)
            pack(zs.at[m, 0], xsum[m, 0])
            copy = send(remote(("z", 0, m), zs.at[m, 0], zr.at[m, 0], zmate))
            yield
            copy.wait_recv()
            total = unpack(zs.at[m, 0], tq, half) + unpack(zr.at[m, 0], tq, half)
        grad_rows = pl.ds(pl.multiple_of(tok * (m % SPLIT) + tq * x, tq), tq)
        gs[m] = (total + gbuf[m // SPLIT, grad_rows, cols(half * core, half)]).astype(BF16)
        for copy in beyond_copies(m):
            send(copy)
        pack(ds.at[m], total)
        send(cross_copy(m))
        out[out_block(m, tq * x, tq)] = total.astype(BF16)
        for _ in range(HOLD * (chunks - 1 - m)):
            yield
        yield from spread(m)

    def cross_copy(m):
        return remote(("cross", m), ds.at[m], bs.at[m], cross)

    def beyond_copies(m):
        return [
            remote(("beyond", i, m), gs.at[m], glow.at[m, b, core, cols(tq * x, tq)], to)
            for i, to in enumerate(beyond)
        ]

    @pl.when(s == 0)
    def _():
        interleave(down_chain, START_DOWN)


    def up_weights():
        for load in v_loads:
            load.wait()

        @pl.loop(0, tile // 128)
        def _(i):
            columns = cols(128 * i, 128)
            stripe[:tile, :] = v_raw[:, columns].astype(F32)
            for q in range(2):
                vt[q, columns, :] = stripe[pl.ds(q, half, stride=2), :].T.astype(BF16)

        w_load.wait()

        @pl.loop(0, half // 128)
        def _(i):
            for q in range(2):
                stripe[pl.ds(q, tile, stride=2), :] = w_raw[:, cols(half * q + 128 * i, 128)].astype(F32)
            wt[cols(128 * i, 128), :] = stripe[...].T.astype(BF16)

    def up_chain(m):
        for copy in beyond_copies(m):
            copy.wait_recv()
        copies = yield from ring_gather("g", m, lambda start, size: glow.at[m, :, core, cols(start, size)], DIRECT)
        for copy in copies:
            copy.wait_recv()
        swaps = []
        for part in range(2):
            columns = pl.ds(fourth * part, fourth)
            total = None
            for q in range(2):
                for k in range(2):
                    term = dot_nn(glow[m, q, k], vt[q, k * half : (k + 1) * half, columns])
                    total = term if total is None else total + term
            pf[m, :, columns] = total
            pack(sb.at[m, part, 0], total[:th])
            one = send(remote(("p1u", m, part), sb.at[m, part, 0], rl.at[m, part, 0], up))
            pack(sb.at[m, part, 1], total[th:])
            two = send(remote(("p1d", m, part), sb.at[m, part, 1], rl.at[m, part, 1], down))
            swaps.append((one, two))
        yield
        relayed = []
        for part, (one, two) in enumerate(swaps):
            one.wait_recv()
            three = remote(("p2u", m, part), rl.at[m, part, 0], rp.at[m, part, 0], up)
            relayed.append(send(three))
            two.wait_recv()
            four = remote(("p2d", m, part), rl.at[m, part, 1], rp.at[m, part, 1], down)
            relayed.append(send(four))
        yield
        for copy in relayed:
            copy.wait_recv()
        for part in range(2):
            columns = pl.ds(fourth * part, fourth)
            came = [unpack(rp.at[m, part, i], th, fourth) for i in range(2)]
            total = pf[m, :, columns] + jnp.concatenate(came, axis=0)
            hid[m, :, columns] = (total * prev[m, :, columns]).astype(BF16)

        def product(q, k):
            pb[m, q, k] = dot_nn(hid[m, :, :half], wt[:, cols(tile * q + half * k, half)])

        copies = []
        for q in range(2):
            product(q, 1 - core)
            copies.append(core_send(m, q))
        for q in range(2):
            product(q, core)
        yield
        for copy in copies:
            copy.wait_recv()
        first = x_first(m, 2)
        yield
        second = x_second(m, 2, first)
        yield
        x_last(m, 2, second)
        pack(zs.at[m, 1], xsum[m, 1 - b])
        copies = [send(remote(("z", i, m), zs.at[m, 1], zr.at[m, i], to)) for i, to in ((2, corner), (1, wmate))]
        pack(zs.at[m, 0], xsum[m, b])
        copies.append(send(remote(("z", 0, m), zs.at[m, 0], zr.at[m, 0], zmate)))
        yield
        for copy in copies:
            copy.wait_recv()
        cross_copy(m).wait_recv()
        terms = [unpack(part, tq, half) for part in (zs.at[m, 0], zr.at[m, 0], zr.at[m, 1], zr.at[m, 2])]
        total = (terms[0] + terms[1]) + (terms[2] + terms[3])
        out[out_block(m, tq * x, tq)] = (total + unpack(bs.at[m], tq, half)).astype(BF16)
        yield from spread(m)

    @pl.when(s == 1)
    def _():
        up_weights()
        all_in()
        for m in range(chunks):
            pre_up[m].wait()
            slope_stage(m, half)
        interleave(up_chain, START_UP)


def local(grad_out, weight_in, weight_out, pre_act):
    batches, tok, tile = grad_out.shape
    chunks, whole, tok = batches * SPLIT, tok, tok // SPLIT
    half, fourth = tile // 2, tile // 4
    th, tq = tok // 2, tok // 4
    vmem = pltpu.VMEM
    scratch = [
        vmem((tile, tile), BF16),
        vmem((tile, tile), BF16),
        vmem((2, tile, half), BF16),
        vmem((half, 2 * tile), BF16),
        vmem((2 * tile, 128), F32),
        vmem((batches, whole, tile), F32),
        vmem((batches, 2, whole, half), BF16),
        vmem((chunks, 2, 2, tok, half), BF16),
        vmem((chunks, tq, half), BF16),
        vmem((chunks, tok, half), F32),
        vmem((batches, 4, whole, fourth), F32),
        vmem((chunks, 2, th * fourth // 128 + 16, 128), BF16),
        vmem((chunks, 2, tok * fourth // 128 + 16, 128), BF16),
        vmem((chunks, 2, th * fourth // 128 + 16, 128), BF16),
        vmem((chunks, 2, tok * fourth // 128 + 16, 128), BF16),
        vmem((chunks, tok, tile), BF16),
        vmem((chunks, tok, half), F32),
        vmem((chunks, 2, 2, th * fourth // 128 + 16, 128), BF16),
        vmem((chunks, 2, 2, th * fourth // 128 + 16, 128), BF16),
        vmem((chunks, 2, 2, th * fourth // 128 + 16, 128), BF16),
        vmem((chunks, 2, 2, tok, half), F32),
        vmem((chunks, 2, tok, half), F32),
        vmem((chunks, 2, tq * half // 128 + 16, 128), BF16),
        vmem((chunks, 2, tq * tile // 128 + 16, 128), BF16),
        vmem((chunks, 2, tq * half // 128 + 16, 128), BF16),
        vmem((chunks, 2, tq * tile // 128 + 16, 128), BF16),
        vmem((chunks, 2, tq * half // 128 + 16, 128), BF16),
        vmem((chunks, 2, tq, half), F32),
        vmem((chunks, 2, tq * half // 128 + 16, 128), BF16),
        vmem((chunks, 3, tq * half // 128 + 16, 128), BF16),
        vmem((chunks, tq * half // 128 + 16, 128), BF16),
        vmem((chunks, tq * half // 128 + 16, 128), BF16),
        pltpu.SemaphoreType.DMA((N_REMOTE,)),
        pltpu.SemaphoreType.DMA((N_REMOTE,)),
        pltpu.SemaphoreType.DMA((N_LOCAL,)),
    ]
    anywhere = pl.BlockSpec(memory_space=pl.ANY)
    change = pl.pallas_call(
        kernel,
        out_shape=vmem((1, batches, whole, tile), BF16),
        in_specs=[anywhere] * 4,
        out_specs=pl.BlockSpec(memory_space=vmem),
        scratch_shapes=scratch,
        compiler_params=pltpu.CompilerParams(
            collective_id=0, has_side_effects=True, vmem_limit_bytes=60_000_000
        ),
    )(grad_out, weight_in, weight_out, pre_act)
    return grad_out[None] + change.astype(F32)


def solution(mesh):
    return jax.shard_map(
        local,
        mesh=mesh,
        in_specs=(
            P(None, None, "wid"),
            P("section", "wid", "hid"),
            P("section", "hid", "wid"),
            P("section", None, None, "hid"),
        ),
        out_specs=P("section", None, None, "wid"),
        check_vma=False,
    )
```
